256 devices in a mesh: date: 8 (over y, core), tile: 32 (over x, z).
Axes of the slice: x: 4, y: 4, z: 8, core: 2. Of those that a mesh axis runs over, the one named last changes fastest.
Arguments:
- radar_echoes: bfloat16 [2048, 16, 32, 2, 256], P('tile', None, 'date')
- destination_panel: int32 [2048, 1], P('tile'), may hold values from 0 to 31; in each aligned block of 64 rows (0 to 63, 64 to 127, ...) at most 3 rows name the same one
- panel_line_shift: int32 [2048], P('tile'), may hold values from 0 to 240
- epoch_couples: int32 [64, 2], replicated, may hold values from 0 to 31, as said below
Outputs:
- coherence: float32 [8192, 64, 256], P('tile', 'date')
The draws below stay inside these ranges and needn't reach their ends.
Inputs may be any that keep to these rules, and one draw needn't show every extreme that they name: `destination_panel`: of the blocks held by one index of tile, at most 3 land on the same tile; some index reaches it. `epoch_couples`: each row names an earlier date and a later one, 1 to 3 dates apart.
All inputs are finite; a program needn't handle non-finite values.
Results may differ from the reference program's by a relative error of at most 0.00079.
Values may be sent and summed in bfloat16 or wider, within the bound.
A program may use at most 64 MiB of HBM per device.

```python
import math
import jax
import jax.numpy as jnp
import numpy as np
from jax import lax

TC = 256
BR = 16
TR = 256
BLK_DEV = 64
CAP = 3
SRC_BLOCKS = 2048
DATES = 32
PAIRS = 64
N_TILE = 32


def draw_radar_echoes(key, part):
    common = jax.random.normal(jax.random.fold_in(key, 11), (SRC_BLOCKS, BR, 1, 2, TC), jnp.float32)
    own = jax.random.normal(jax.random.fold_in(key, 12), (SRC_BLOCKS, BR, DATES, 2, TC), jnp.float32)
    rho = jax.random.uniform(jax.random.fold_in(key, 13), (SRC_BLOCKS, 1, DATES, 1, 1), jnp.float32, 0.2, 0.95)
    amplitude = jax.random.uniform(jax.random.fold_in(key, 14), (SRC_BLOCKS, BR, 1, 1, TC), jnp.float32, 0.5, 1.5)
    value = amplitude * (rho * common + jnp.sqrt(1.0 - rho * rho) * own)
    value = jnp.clip(value, -40.0, 40.0)
    return value.astype(jnp.bfloat16)


def draw_epoch_couples(key, part):
    spacing = jax.random.randint(jax.random.fold_in(key, 21), (PAIRS,), 1, 4)
    earlier = jax.random.randint(jax.random.fold_in(key, 22), (PAIRS,), 0, DATES - 3)
    places = jnp.arange(PAIRS)
    earlier = jnp.where(places == 0, DATES - 1 - spacing, earlier)
    earlier = jnp.where(places == 1, 0, earlier)
    return jnp.stack([earlier, earlier + spacing], axis=1).astype(jnp.int32)


def place_ends(values, own_key, low, top_value):
    index_at = [jax.random.randint(jax.random.fold_in(own_key, axis), (), 0, length) for axis, length in enumerate(values.shape)]
    widest = values.shape.index(max(values.shape))
    neighbour = index_at[:widest] + [(index_at[widest] + 1) % values.shape[widest]] + index_at[widest + 1:]
    return values.at[tuple(index_at)].set(low).at[tuple(neighbour)].set(top_value)


def assign_block(rng, own, number, rows, number_of, top, bound, lean):
    order = jax.random.permutation(rng, number_of)
    packed, ordinary = shares(number_of, rows * top, bound, lean, True), shares(number_of, rows * top, bound, lean, False)
    places = jnp.arange(number_of)

    def named(lengths, turn):
        used = int((lengths > 0).sum())
        fixed = max(1, used // 4)
        moved = fixed + (places - fixed + turn * (used - fixed)) % max(1, number_of - fixed)
        return jnp.zeros((number_of,), jnp.int32).at[order[jnp.where(places < fixed, places, moved)]].set(jnp.asarray(lengths, jnp.int32))

    lengths = jnp.where(number % 4 == 0, named(packed, number // 4), named(ordinary, number - number // 4 - 1))
    mixed = jax.random.permutation(jax.random.fold_in(own, 3), number_of)
    giver, receiver = mixed[0:number_of // 2 * 2:2], mixed[1:number_of // 2 * 2:2]
    room = jnp.minimum(lengths[giver] - 1, bound - lengths[receiver]) // 2
    room = jnp.where((giver == order[0]) | (receiver == order[0]) | (lengths[receiver] == 0), 0, jnp.maximum(room, 0))
    moved = jax.random.randint(jax.random.fold_in(own, 4), (number_of // 2,), 0, 1 << 20) % (room + 1)
    lengths = lengths.at[giver].add(-moved).at[receiver].add(moved)
    items = jnp.searchsorted(jnp.cumsum(lengths), jnp.arange(rows * top), side="right").astype(jnp.int32)
    table = items.reshape(top, rows).T
    table = table[jax.random.permutation(jax.random.fold_in(own, 1), rows)]
    turn = jax.random.randint(jax.random.fold_in(own, 2), (rows, 1), 0, top)
    return jnp.take_along_axis(table, (jnp.arange(top)[None, :] + turn) % top, axis=1)


def shares(count, total, reach, lean, full):
    weights = [(1 << 20) // math.isqrt(standing ** lean) + 1 for standing in range(1, count + 1)]
    largest = reach if full else min(reach, max(-(-total // count), total * weights[0] // sum(weights)))
    least = 1 if total - largest >= count - 1 else 0
    holding, spare = [largest] + [least] * (count - 1), total - largest - least * (count - 1)
    while spare > 0:
        movable = [i for i in range(1, count) if holding[i] < largest] or [i for i in range(1, count) if holding[i] < reach]
        mass, left = sum([weights[i] for i in movable]), spare
        for i in movable:
            extra = min(reach - holding[i], max(1, left * weights[i] // mass), spare)
            holding[i] = holding[i] + extra
            spare = spare - extra
    return np.array(holding)


def setup_inputs(seed: int = 0) -> dict:
    streams_of = jax.random.split(jax.random.key(seed), 5)
    radar_echoes = draw_radar_echoes(jax.random.fold_in(streams_of[4], 71), 0)
    destination_panel_keys = jax.random.split(jax.random.fold_in(streams_of[1], 1), SRC_BLOCKS // BLK_DEV)
    destination_panel_turns = jax.random.permutation(jax.random.fold_in(streams_of[1], 3), SRC_BLOCKS // BLK_DEV)
    destination_panel = jax.vmap(lambda own, number: assign_block(jax.random.fold_in(streams_of[1], 2), own, number, BLK_DEV, N_TILE, 1, CAP, 2))(destination_panel_keys, destination_panel_turns).reshape((SRC_BLOCKS, 1))
    panel_line_shift = place_ends(jax.random.randint(streams_of[2], (SRC_BLOCKS,), 0, TR - BR + 1), jax.random.fold_in(streams_of[2], 1), 0, TR - BR).astype(jnp.int32)
    epoch_couples = draw_epoch_couples(jax.random.fold_in(streams_of[4], 71), 0)
    return {"radar_echoes": radar_echoes, "destination_panel": destination_panel, "panel_line_shift": panel_line_shift, "epoch_couples": epoch_couples}


def window_sum(field, rows):
    total = field[0:rows]
    for row_lag in range(1, 7):
        total = total + field[row_lag:row_lag + rows]
    cols = total.shape[-1]
    padded = jnp.pad(total, ((0, 0), (0, 0), (7, 7)))
    result = padded[..., 0:cols]
    for column_lag in range(1, 15):
        result = result + padded[..., column_lag:column_lag + cols]
    return result

def coherence_of(first, second, rows):
    first = first.astype(jnp.float32)
    second = second.astype(jnp.float32)
    first_re, first_im = (first[:, :, 0], first[:, :, 1])
    second_re, second_im = (second[:, :, 0], second[:, :, 1])
    cross_re = first_re * second_re + first_im * second_im
    cross_im = first_im * second_re - first_re * second_im
    power_a = first_re * first_re + first_im * first_im
    power_e = second_re * second_re + second_im * second_im
    box_re = window_sum(cross_re, rows)
    box_im = window_sum(cross_im, rows)
    box_a = window_sum(power_a, rows)
    box_e = window_sum(power_e, rows)
    return jnp.sqrt(box_re * box_re + box_im * box_im) / jnp.sqrt(jnp.maximum(box_a * box_e, 1.0))

def reference(radar_echoes, destination_panel, panel_line_shift, epoch_couples):
    opening_lines = (destination_panel[:, 0] * TR + panel_line_shift).astype(jnp.int32)
    panel_raster = jnp.zeros((N_TILE * TR, DATES, 2, TC), jnp.float32)

    def deposit_patch(carry, item):
        block, start = item
        current = lax.dynamic_slice_in_dim(carry, start, BR, 0)
        return (lax.dynamic_update_slice_in_dim(carry, current + block.astype(jnp.float32), start, 0), None)
    panel_raster, ignored_value = lax.scan(deposit_patch, panel_raster, (radar_echoes, opening_lines))
    panel_raster = panel_raster.astype(jnp.bfloat16).reshape(N_TILE, TR, DATES, 2, TC)
    panel_raster = jnp.transpose(panel_raster, (1, 0, 2, 3, 4))
    panel_raster = jnp.pad(panel_raster, ((3, 3), (0, 0), (0, 0), (0, 0), (0, 0)))

    def one_pair(pair_row):
        first = lax.dynamic_index_in_dim(panel_raster, pair_row[0], axis=2, keepdims=False)
        second = lax.dynamic_index_in_dim(panel_raster, pair_row[1], axis=2, keepdims=False)
        return coherence_of(first, second, TR)
    result = lax.map(one_pair, epoch_couples)
    result = jnp.transpose(result, (2, 1, 0, 3))
    return result.reshape(N_TILE * TR, PAIRS, TC)
```

```python
import functools

import jax
import jax.numpy as jnp
from jax import lax
from jax.experimental import pallas as pl
from jax.experimental.pallas import tpu as pltpu
from jax.sharding import PartitionSpec as P

NX, NZ, NY = 4, 8, 4
NT = NX * NZ
TR = 256
BR = 16
CAP = 3
BLK = 64
NQ = 8
KS = CAP * BR * 2
KP = 128
NP = 8
MSG = 2 * TR + 16
LEVELS = 32000.0
MESH = pl.DeviceIdType.MESH


def sort_kernel(dest, shift, x_ref, z_ref, koff_ref, held, zeros, count, block_of, in_sem, out_sem):
    loads = []
    for q in range(NQ):
        half, date = divmod(q, 4)
        copy = pltpu.make_async_copy(
            x_ref.at[:, :, date, :, pl.ds(half * 128, 128)], held.at[q], in_sem.at[q]
        )
        copy.start()
        loads.append(copy)
    zeros[...] = jnp.zeros_like(zeros)

    @pl.loop(0, NT)
    def _(t):
        count[t] = 0

    @pl.loop(0, NT * CAP)
    def _(s):
        block_of[s] = -1

    @pl.loop(0, BLK)
    def _(b):
        t = dest[b]
        k = count[t]
        count[t] = k + 1
        block_of[t * CAP + k] = b

    lane = lax.broadcasted_iota(jnp.int32, (1, 128), 1)
    slot = lane >> 5
    inside = ((lane & 31) >> 1) + TR * (lane & 1)

    @pl.loop(0, NT)
    def _(t):
        value = jnp.full((1, 128), -1, jnp.int32)
        for k in range(CAP):
            b = block_of[t * CAP + k]
            start = jnp.where(b >= 0, shift[jnp.maximum(b, 0)], -4096)
            value = jnp.where(slot == k, start + inside, value)
        koff_ref[pl.ds(t, 1), :] = value

    for copy in loads:
        copy.wait()

    @pl.loop(0, NT * CAP)
    def _(s):
        b = block_of[s]

        @pl.when(b >= 0)
        def _():
            pltpu.make_async_copy(held.at[:, b], z_ref.at[:, s], out_sem).start()

        @pl.when(b < 0)
        def _():
            pltpu.make_async_copy(zeros, z_ref.at[:, s], out_sem).start()

    pltpu.make_async_copy(z_ref, z_ref, out_sem).wait()


def sort_blocks(x, dest, shift):
    return pl.pallas_call(
        sort_kernel,
        out_shape=(
            jax.ShapeDtypeStruct((NQ, NT * CAP, BR, 2, 128), jnp.bfloat16),
            jax.ShapeDtypeStruct((NT, 128), jnp.int32),
        ),
        in_specs=[
            pl.BlockSpec(memory_space=pltpu.SMEM),
            pl.BlockSpec(memory_space=pltpu.SMEM),
            pl.BlockSpec(memory_space=pl.ANY),
        ],
        out_specs=(pl.BlockSpec(memory_space=pl.ANY), pl.BlockSpec(memory_space=pltpu.VMEM)),
        scratch_shapes=[
            pltpu.VMEM((NQ, BLK, BR, 2, 128), jnp.bfloat16),
            pltpu.VMEM((NQ, BR, 2, 128), jnp.bfloat16),
            pltpu.SMEM((NT,), jnp.int32),
            pltpu.SMEM((NT * CAP,), jnp.int32),
            pltpu.SemaphoreType.DMA((NQ,)),
            pltpu.SemaphoreType.DMA,
        ],
        name="sort_blocks",
    )(dest, shift, x)


def encode(total, out, rows):
    top = jnp.maximum(jnp.max(rows, axis=0, keepdims=True), 1e-30)
    power = jnp.clip(jnp.ceil(jnp.log2(top)), -100.0, 100.0)
    out[2 * TR :, :] = jnp.broadcast_to(power, (16, 128)).astype(jnp.int32).astype(jnp.int16)
    scale = jnp.exp2(-power)
    for i in range(4):
        v = total[i * 128 : (i + 1) * 128, :]
        y = jnp.abs(v) * scale
        y = y * lax.rsqrt(jnp.maximum(y, 1e-30))
        y = y * lax.rsqrt(jnp.maximum(y, 1e-15))
        m = (y * LEVELS + 0.5).astype(jnp.int32)
        out[i * 128 : (i + 1) * 128, :] = jnp.where(v < 0, -m, m).astype(jnp.int16)


def scale_of(msg):
    power = msg[2 * TR :, :].astype(jnp.int32).astype(jnp.float32)
    return jnp.exp2(power[0:1, :])


def decode(msg, scale, i):
    f = msg[i * 128 : (i + 1) * 128, :].astype(jnp.int32).astype(jnp.float32) * (1.0 / LEVELS)
    f = f * jnp.abs(f)
    f = f * jnp.abs(f)
    return f * scale


def main_kernel(
    z_ref, koff_ref, ep_ref, out_ref,
    got, kof, place, sent, came, total, fall0, fall1, prod, split, acc, bands, result,
    own_sem, xs_sem, xr_sem, zs_sem, zr_sem, ys_sem, yr_sem, cs_sem, cr_sem, ks_sem, kr_sem, out_sem,
):
    d = lax.axis_index("date")
    t = lax.axis_index("tile")
    y, core = d // 2, d % 2
    x, z = t // NZ, t % NZ
    partner = (y * 2 + 1 - core, t)

    def at_x(k):
        return (d, lax.rem(x + k, NX) * NZ + z)

    def at_z(k):
        return (d, x * NZ + lax.rem(z + k + NZ, NZ))

    def at_y(k):
        return (lax.rem(y + k, NY) * 2 + core, t)

    for q in range(NQ):
        @pl.loop(0, NZ)
        def _(j, q=q):
            for s in range(NX):
                got[q, j, s * KP + KS : (s + 1) * KP, :] = jnp.zeros((KP - KS, 128), jnp.bfloat16)

    barrier = pltpu.get_barrier_semaphore()
    peers = [at_x(1), at_x(2), at_x(3), at_z(1), at_z(-1), at_y(1), at_y(2), at_y(3), partner]
    for peer in peers:
        pl.semaphore_signal(barrier, 1, device_id=peer, device_id_type=MESH)
    pl.semaphore_wait(barrier, len(peers))

    def remote(src, dst, ssem, rsem, dev):
        return pltpu.make_async_remote_copy(
            src_ref=src, dst_ref=dst, send_sem=ssem, recv_sem=rsem, device_id=dev, device_id_type=MESH
        )

    def koff_copy(k):
        there = lax.rem(x + k, NX)
        return remote(
            koff_ref.at[pl.ds(pl.multiple_of(there * NZ, NZ), NZ)], kof.at[x],
            ks_sem.at[k - 1], kr_sem.at[k - 1], at_x(k),
        )

    def x_copy(q, k):
        there = lax.rem(x + k, NX)
        return remote(
            z_ref.at[q, pl.ds(there * NZ, NZ)], got.at[q, :, pl.ds(pl.multiple_of(x * KP, KP), KS)],
            xs_sem.at[q, k - 1], xr_sem.at[q, k - 1], at_x(k),
        )

    def own_copy(q):
        return pltpu.make_async_copy(
            z_ref.at[q, pl.ds(x * NZ, NZ)], got.at[q, :, pl.ds(pl.multiple_of(x * KP, KP), KS)],
            own_sem.at[q],
        )

    for k in (1, 3, 2):
        koff_copy(k).start()

    @pl.loop(0, NQ)
    def _(q):
        for k in (1, 3, 2):
            x_copy(q, k).start()
        own_copy(q).start()

    for half in range(2):
        i = lax.broadcasted_iota(jnp.int32, (256, 256), 0)
        j = lax.broadcasted_iota(jnp.int32, (256, 256), 1)
        near = jnp.abs((i & 127) + half * 128 - j) <= 7
        bands[half] = jnp.where(near, 1.0, 0.0).astype(jnp.bfloat16)
    prod[...] = jnp.zeros_like(prod)
    kof[x] = koff_ref[pl.ds(pl.multiple_of(x * NZ, NZ), NZ), :]
    for k in (1, 3, 2):
        koff_copy(k).wait()

    @pl.loop(0, NZ)
    def _(j):
        for s in range(NX):
            goal = kof[s, pl.ds(j, 1), :]
            for i in range(4):
                row = lax.broadcasted_iota(jnp.int32, (128, 128), 0) + i * 128
                hit = jnp.where(row == goal, 1.0, 0.0).astype(jnp.bfloat16)
                place[j, i * 128 : (i + 1) * 128, s * 128 : (s + 1) * 128] = hit

    def part(q, j, i):
        return jnp.dot(
            place[j, i * 128 : (i + 1) * 128, :], got[q, j], preferred_element_type=jnp.float32
        )

    def z_copy(q, n, way):
        dev = (d, x * NZ + lax.rem(z + way + NZ, NZ))
        return remote(sent.at[q, n], came.at[q, n], zs_sem.at[q, n], zr_sem.at[q, n], dev)

    def begin(q, way, dist, n):
        j = lax.rem(z + way * dist + NZ, NZ)
        top = jnp.zeros((8, 128), jnp.float32)
        for i in range(4):
            v = part(q, j, i)
            total[i * 128 : (i + 1) * 128, :] = v
            top = jnp.maximum(top, jnp.max(jnp.abs(v).reshape(16, 8, 128), axis=0))
        encode(total, sent.at[q, n], top)
        z_copy(q, n, way).start()

    def carry_on(q, way, dist, n):
        j = lax.rem(z + way * dist + NZ, NZ)
        z_copy(q, n - 1, way).wait_recv()
        msg = came.at[q, n - 1]
        scale = scale_of(msg)
        top = jnp.zeros((8, 128), jnp.float32)
        for i in range(4):
            v = part(q, j, i) + decode(msg, scale, i)
            total[i * 128 : (i + 1) * 128, :] = v
            top = jnp.maximum(top, jnp.max(jnp.abs(v).reshape(16, 8, 128), axis=0))
        encode(total, sent.at[q, n], top)
        z_copy(q, n, way).start()

    def way_of(q):
        return 1 - 2 * lax.rem(q, 2)

    def y_copy(fall, q, k):
        mine = fall.at[d * 4 + lax.rem(q, 4)]
        return remote(mine, mine, ys_sem.at[q, k - 1], yr_sem.at[q, k - 1], at_y(k))

    def core_copy(fall, q, k):
        from_d = lax.rem(y - k + NY, NY) * 2 + core
        field = fall.at[from_d * 4 + lax.rem(q, 4)]
        return remote(field, field, cs_sem.at[q, k], cr_sem.at[q, k], partner)

    def finish(q, fall):
        way = way_of(q)
        z_copy(q, 3, way).wait_recv()
        z_copy(q, 6, -way).wait_recv()
        one, two = came.at[q, 3], came.at[q, 6]
        s1, s2 = scale_of(one), scale_of(two)
        for i in range(4):
            v = part(q, z, i) + (decode(one, s1, i) + decode(two, s2, i))
            fall[d * 4 + lax.rem(q, 4), i * 128 : (i + 1) * 128, :] = v.astype(jnp.bfloat16)
        for k in (1, 3, 2):
            y_copy(fall, q, k).start()
        core_copy(fall, q, 0).start()

    def forward(q, fall):
        for k in (1, 3, 2):
            y_copy(fall, q, k).wait_recv()
            core_copy(fall, q, k).start()

    def arrive(q, fall):
        for k in range(NY):
            core_copy(fall, q, k).wait_recv()

    def out_copy(side):
        return pltpu.make_async_copy(
            result.reshape(2, TR, NP, 128).at[side],
            out_ref.at[:, :, pl.ds(side * 128, 128)],
            out_sem.at[side],
        )

    def boxes(half, fall):
        @pl.loop(0, NP)
        def _(p):
            a = ep_ref[d * NP + p, 0]
            e = ep_ref[d * NP + p, 1]
            for i in range(4):
                lo = i * 64
                u0 = fall[a, lo : lo + 64, :].astype(jnp.float32)
                u1 = fall[a, TR + lo : TR + lo + 64, :].astype(jnp.float32)
                v0 = fall[e, lo : lo + 64, :].astype(jnp.float32)
                v1 = fall[e, TR + lo : TR + lo + 64, :].astype(jnp.float32)
                prod[0, 8 + lo : 72 + lo, :] = u0 * v0 + u1 * v1
                prod[1, 8 + lo : 72 + lo, :] = u1 * v0 - u0 * v1
                prod[2, 8 + lo : 72 + lo, :] = u0 * u0 + u1 * u1
                prod[3, 8 + lo : 72 + lo, :] = v0 * v0 + v1 * v1
            for f in range(4):
                for i in range(4):
                    lo = i * 64
                    s = prod[f, 5 + lo : 69 + lo, :]
                    for k in range(1, 7):
                        s = s + prod[f, 5 + lo + k : 69 + lo + k, :]
                    high = s.astype(jnp.bfloat16)
                    split[f, lo : lo + 64, 0:128] = high
                    split[f, lo : lo + 64, 128:256] = (s - high.astype(jnp.float32)).astype(jnp.bfloat16)
            for f in range(4):
                r = jnp.dot(split[f], bands[half], preferred_element_type=jnp.float32)
                acc[p, f] = r if half == 0 else acc[p, f] + r
            if half == 1:
                for i in range(8):
                    lo = i * 32
                    re, im = acc[p, 0, lo : lo + 32, :], acc[p, 1, lo : lo + 32, :]
                    pa, pe = acc[p, 2, lo : lo + 32, :], acc[p, 3, lo : lo + 32, :]
                    c = jnp.sqrt(re * re + im * im) / jnp.sqrt(jnp.maximum(pa * pe, 1.0))
                    for side in range(2):
                        rows = pl.ds(side * NP * TR + lo * NP + p, 32, stride=NP)
                        result[rows, :] = c[:, side * 128 : (side + 1) * 128]

    @pl.loop(0, NQ + 6)
    def _(step):
        @pl.when(step < NQ)
        def _():
            q = step
            for k in (1, 3, 2):
                x_copy(q, k).wait_recv()
            own_copy(q).wait()
            begin(q, way_of(q), 4, 0)

        @pl.when((step >= 1) & (step < NQ + 1))
        def _():
            q = step - 1
            begin(q, -way_of(q), 3, 4)

        @pl.loop(0, 5)
        def _(i):
            short = i // 3
            h = i + 1 - 2 * short
            q = step - h

            @pl.when((q >= 0) & (q < NQ))
            def _():
                carry_on(q, way_of(q) * (1 - 2 * short), 4 - h, h + 3 * short)

        for half, fall in enumerate((fall0, fall1)):
            first = half * 4

            @pl.when((step >= first + 4) & (step < first + 8))
            def _(fall=fall):
                finish(step - 4, fall)

            @pl.when((step >= first + 5) & (step < first + 9))
            def _(fall=fall):
                forward(step - 5, fall)

            @pl.when((step >= first + 6) & (step < first + 10))
            def _(fall=fall):
                arrive(step - 6, fall)

        @pl.when(step == 9)
        def _():
            boxes(0, fall0)

    boxes(1, fall1)
    for side in range(2):
        out_copy(side).start()

    @pl.loop(0, NQ)
    def _(q):
        for k in (1, 3, 2):
            x_copy(q, k).wait_send()
        for n in range(7):
            z_copy(q, n, 1).wait_send()
        for k in (1, 2, 3):
            y_copy(fall0, q, k).wait_send()
        for k in range(NY):
            core_copy(fall0, q, k).wait_send()

    for side in range(2):
        out_copy(side).wait()


def main_call(z, koff, epochs):
    dma = pltpu.SemaphoreType.DMA
    field = pltpu.VMEM((32, 2 * TR, 128), jnp.bfloat16)
    return pl.pallas_call(
        main_kernel,
        out_shape=jax.ShapeDtypeStruct((TR, NP, 256), jnp.float32),
        in_specs=[
            pl.BlockSpec(memory_space=pl.ANY),
            pl.BlockSpec(memory_space=pltpu.VMEM),
            pl.BlockSpec(memory_space=pltpu.SMEM),
        ],
        out_specs=pl.BlockSpec(memory_space=pl.ANY),
        scratch_shapes=[
            pltpu.VMEM((NQ, NZ, NX * KP, 128), jnp.bfloat16),
            pltpu.VMEM((NX, NZ, 128), jnp.int32),
            pltpu.VMEM((NZ, 2 * TR, NX * KP), jnp.bfloat16),
            pltpu.VMEM((NQ, 7, MSG, 128), jnp.int16),
            pltpu.VMEM((NQ, 7, MSG, 128), jnp.int16),
            pltpu.VMEM((2 * TR, 128), jnp.float32),
            field,
            field,
            pltpu.VMEM((4, TR + 16, 128), jnp.float32),
            pltpu.VMEM((4, TR, 256), jnp.bfloat16),
            pltpu.VMEM((NP, 4, TR, 256), jnp.float32),
            pltpu.VMEM((2, 256, 256), jnp.bfloat16),
            pltpu.VMEM((2 * TR * NP, 128), jnp.float32),
            dma((NQ,)),
            dma((NQ, 3)), dma((NQ, 3)),
            dma((NQ, 7)), dma((NQ, 7)),
            dma((NQ, 3)), dma((NQ, 3)),
            dma((NQ, NY)), dma((NQ, NY)),
            dma((3,)), dma((3,)),
            dma((2,)),
        ],
        compiler_params=pltpu.CompilerParams(
            collective_id=0, has_side_effects=True, vmem_limit_bytes=62 * 2**20
        ),
        name="tiles_and_coherence",
    )(z, koff, epochs)


def local(radar_echoes, destination_panel, panel_line_shift, epoch_couples):
    z, koff = sort_blocks(radar_echoes, destination_panel[:, 0], panel_line_shift)
    z = z.reshape(NQ, NT, KS, 128)
    return main_call(z, koff, epoch_couples)


def solution(mesh):
    in_specs = (P("tile", None, "date", None, None), P("tile", None), P("tile"), P())
    out_specs = P("tile", "date", None)
    return jax.shard_map(local, mesh=mesh, in_specs=in_specs, out_specs=out_specs, check_vma=False)
```

```python
import functools

import jax
import jax.numpy as jnp
from jax import lax
from jax.experimental import pallas as pl
from jax.experimental.pallas import tpu as pltpu
from jax.sharding import PartitionSpec as P

NX, NZ, NY = 4, 8, 4
NT = NX * NZ
TR = 256
BR = 16
CAP = 3
BLK = 64
NQ = 8
KS = CAP * BR * 2
KP = 128
NP = 8
MSG = 2 * TR + 16
LEVELS = 32000.0
MESH = pl.DeviceIdType.MESH


def sort_kernel(dest, shift, x_ref, z_ref, koff_ref, held, zeros, count, block_of, in_sem, out_sem):
    loads = []
    for q in range(NQ):
        half, date = divmod(q, 4)
        copy = pltpu.make_async_copy(
            x_ref.at[:, :, date, :, pl.ds(half * 128, 128)], held.at[q], in_sem.at[q]
        )
        copy.start()
        loads.append(copy)
    zeros[...] = jnp.zeros_like(zeros)

    @pl.loop(0, NT)
    def _(t):
        count[t] = 0

    @pl.loop(0, NT * CAP)
    def _(s):
        block_of[s] = -1

    @pl.loop(0, BLK)
    def _(b):
        t = dest[b]
        k = count[t]
        count[t] = k + 1
        block_of[t * CAP + k] = b

    lane = lax.broadcasted_iota(jnp.int32, (1, 128), 1)
    slot = lane >> 5
    inside = ((lane & 31) >> 1) + TR * (lane & 1)

    @pl.loop(0, NT)
    def _(t):
        value = jnp.full((1, 128), -1, jnp.int32)
        for k in range(CAP):
            b = block_of[t * CAP + k]
            start = jnp.where(b >= 0, shift[jnp.maximum(b, 0)], -4096)
            value = jnp.where(slot == k, start + inside, value)
        koff_ref[pl.ds(t, 1), :] = value

    for copy in loads:
        copy.wait()

    @pl.loop(0, NT * CAP)
    def _(s):
        b = block_of[s]

        @pl.when(b >= 0)
        def _():
            pltpu.make_async_copy(held.at[:, b], z_ref.at[:, s], out_sem).start()

        @pl.when(b < 0)
        def _():
            pltpu.make_async_copy(zeros, z_ref.at[:, s], out_sem).start()

    pltpu.make_async_copy(z_ref, z_ref, out_sem).wait()


def sort_blocks(x, dest, shift):
    return pl.pallas_call(
        sort_kernel,
        out_shape=(
            jax.ShapeDtypeStruct((NQ, NT * CAP, BR, 2, 128), jnp.bfloat16),
            jax.ShapeDtypeStruct((NT, 128), jnp.int32),
        ),
        in_specs=[
            pl.BlockSpec(memory_space=pltpu.SMEM),
            pl.BlockSpec(memory_space=pltpu.SMEM),
            pl.BlockSpec(memory_space=pl.ANY),
        ],
        out_specs=(pl.BlockSpec(memory_space=pl.ANY), pl.BlockSpec(memory_space=pltpu.VMEM)),
        scratch_shapes=[
            pltpu.VMEM((NQ, BLK, BR, 2, 128), jnp.bfloat16),
            pltpu.VMEM((NQ, BR, 2, 128), jnp.bfloat16),
            pltpu.SMEM((NT,), jnp.int32),
            pltpu.SMEM((NT * CAP,), jnp.int32),
            pltpu.SemaphoreType.DMA((NQ,)),
            pltpu.SemaphoreType.DMA,
        ],
        name="sort_blocks",
    )(dest, shift, x)


def encode(total, out, rows):
    top = jnp.maximum(jnp.max(rows, axis=0, keepdims=True), 1e-30)
    power = jnp.clip(jnp.ceil(jnp.log2(top)), -100.0, 100.0)
    out[2 * TR :, :] = jnp.broadcast_to(power, (16, 128)).astype(jnp.int32).astype(jnp.int16)
    scale = jnp.exp2(-power)
    for i in range(4):
        v = total[i * 128 : (i + 1) * 128, :]
        y = jnp.abs(v) * scale
        y = y * lax.rsqrt(jnp.maximum(y, 1e-30))
        y = y * lax.rsqrt(jnp.maximum(y, 1e-15))
        m = (y * LEVELS + 0.5).astype(jnp.int32)
        out[i * 128 : (i + 1) * 128, :] = jnp.where(v < 0, -m, m).astype(jnp.int16)


def scale_of(msg):
    power = msg[2 * TR :, :].astype(jnp.int32).astype(jnp.float32)
    return jnp.exp2(power[0:1, :])


def decode(msg, scale, i):
    f = msg[i * 128 : (i + 1) * 128, :].astype(jnp.int32).astype(jnp.float32) * (1.0 / LEVELS)
    f = f * jnp.abs(f)
    f = f * jnp.abs(f)
    return f * scale


def main_kernel(
    z_ref, koff_ref, ep_ref, out_ref,
    got, kof, place, sent, came, total, fall0, fall1, prod, split, acc, bands, result,
    own_sem, xs_sem, xr_sem, zs_sem, zr_sem, ys_sem, yr_sem, cs_sem, cr_sem, ks_sem, kr_sem, out_sem,
):
    d = lax.axis_index("date")
    t = lax.axis_index("tile")
    y, core = d // 2, d % 2
    x, z = t // NZ, t % NZ
    partner = (y * 2 + 1 - core, t)

    def at_x(k):
        return (d, lax.rem(x + k, NX) * NZ + z)

    def at_z(k):
        return (d, x * NZ + lax.rem(z + k + NZ, NZ))

    def at_y(k):
        return (lax.rem(y + k, NY) * 2 + core, t)

    for q in range(NQ):
        @pl.loop(0, NZ)
        def _(j, q=q):
            for s in range(NX):
                got[q, j, s * KP + KS : (s + 1) * KP, :] = jnp.zeros((KP - KS, 128), jnp.bfloat16)

    barrier = pltpu.get_barrier_semaphore()
    peers = [at_x(1), at_x(2), at_x(3), at_z(1), at_z(-1), at_y(1), at_y(2), at_y(3), partner]
    for peer in peers:
        pl.semaphore_signal(barrier, 1, device_id=peer, device_id_type=MESH)
    pl.semaphore_wait(barrier, len(peers))

    def remote(src, dst, ssem, rsem, dev):
        return pltpu.make_async_remote_copy(
            src_ref=src, dst_ref=dst, send_sem=ssem, recv_sem=rsem, device_id=dev, device_id_type=MESH
        )

    def koff_copy(k):
        there = lax.rem(x + k, NX)
        return remote(
            koff_ref.at[pl.ds(pl.multiple_of(there * NZ, NZ), NZ)], kof.at[x],
            ks_sem.at[k - 1], kr_sem.at[k - 1], at_x(k),
        )

    def x_copy(q, k):
        there = lax.rem(x + k, NX)
        return remote(
            z_ref.at[q, pl.ds(there * NZ, NZ)], got.at[q, :, pl.ds(pl.multiple_of(x * KP, KP), KS)],
            xs_sem.at[q, k - 1], xr_sem.at[q, k - 1], at_x(k),
        )

    def own_copy(q):
        return pltpu.make_async_copy(
            z_ref.at[q, pl.ds(x * NZ, NZ)], got.at[q, :, pl.ds(pl.multiple_of(x * KP, KP), KS)],
            own_sem.at[q],
        )

    for k in (1, 3, 2):
        koff_copy(k).start()

    @pl.loop(0, NQ)
    def _(q):
        for k in (1, 3, 2):
            x_copy(q, k).start()
        own_copy(q).start()

    for half in range(2):
        i = lax.broadcasted_iota(jnp.int32, (256, 256), 0)
        j = lax.broadcasted_iota(jnp.int32, (256, 256), 1)
        near = jnp.abs((i & 127) + half * 128 - j) <= 7
        bands[half] = jnp.where(near, 1.0, 0.0).astype(jnp.bfloat16)
    prod[...] = jnp.zeros_like(prod)
    kof[x] = koff_ref[pl.ds(pl.multiple_of(x * NZ, NZ), NZ), :]
    for k in (1, 3, 2):
        koff_copy(k).wait()

    @pl.loop(0, NZ)
    def _(j):
        for s in range(NX):
            goal = kof[s, pl.ds(j, 1), :]
            for i in range(4):
                row = lax.broadcasted_iota(jnp.int32, (128, 128), 0) + i * 128
                hit = jnp.where(row == goal, 1.0, 0.0).astype(jnp.bfloat16)
                place[j, i * 128 : (i + 1) * 128, s * 128 : (s + 1) * 128] = hit

    def part(q, j, i):
        return jnp.dot(
            place[j, i * 128 : (i + 1) * 128, :], got[q, j], preferred_element_type=jnp.float32
        )

    def z_copy(q, n, way):
        dev = (d, x * NZ + lax.rem(z + way + NZ, NZ))
        return remote(sent.at[q, n], came.at[q, n], zs_sem.at[q, n], zr_sem.at[q, n], dev)

    def begin(q, way, dist, n):
        j = lax.rem(z + way * dist + NZ, NZ)
        top = jnp.zeros((8, 128), jnp.float32)
        for i in range(4):
            v = part(q, j, i)
            total[i * 128 : (i + 1) * 128, :] = v
            top = jnp.maximum(top, jnp.max(jnp.abs(v).reshape(16, 8, 128), axis=0))
        encode(total, sent.at[q, n], top)
        z_copy(q, n, way).start()

    def carry_on(q, way, dist, n):
        j = lax.rem(z + way * dist + NZ, NZ)
        z_copy(q, n - 1, way).wait_recv()
        msg = came.at[q, n - 1]
        scale = scale_of(msg)
        top = jnp.zeros((8, 128), jnp.float32)
        for i in range(4):
            v = part(q, j, i) + decode(msg, scale, i)
            total[i * 128 : (i + 1) * 128, :] = v
            top = jnp.maximum(top, jnp.max(jnp.abs(v).reshape(16, 8, 128), axis=0))
        encode(total, sent.at[q, n], top)
        z_copy(q, n, way).start()

    def way_of(q):
        return 1 - 2 * lax.rem(q, 2)

    def y_copy(fall, q, k):
        mine = fall.at[d * 4 + lax.rem(q, 4)]
        return remote(mine, mine, ys_sem.at[q, k - 1], yr_sem.at[q, k - 1], at_y(k))

    def core_copy(fall, q, k):
        from_d = lax.rem(y - k + NY, NY) * 2 + core
        field = fall.at[from_d * 4 + lax.rem(q, 4)]
        return remote(field, field, cs_sem.at[q, k], cr_sem.at[q, k], partner)

    def finish(q, fall):
        way = way_of(q)
        z_copy(q, 3, way).wait_recv()
        z_copy(q, 6, -way).wait_recv()
        one, two = came.at[q, 3], came.at[q, 6]
        s1, s2 = scale_of(one), scale_of(two)
        for i in range(4):
            v = part(q, z, i) + (decode(one, s1, i) + decode(two, s2, i))
            fall[d * 4 + lax.rem(q, 4), i * 128 : (i + 1) * 128, :] = v.astype(jnp.bfloat16)
        for k in (1, 3, 2):
            y_copy(fall, q, k).start()
        core_copy(fall, q, 0).start()

    def forward(q, fall):
        for k in (1, 3, 2):
            y_copy(fall, q, k).wait_recv()
            core_copy(fall, q, k).start()

    def arrive(q, fall):
        for k in range(NY):
            core_copy(fall, q, k).wait_recv()

    def out_copy(side):
        return pltpu.make_async_copy(
            result.reshape(2, TR, NP, 128).at[side],
            out_ref.at[:, :, pl.ds(side * 128, 128)],
            out_sem.at[side],
        )

    def boxes(half, fall):
        @pl.loop(0, NP)
        def _(p):
            a = ep_ref[0, d * NP + p]
            e = ep_ref[1, d * NP + p]
            for i in range(4):
                lo = i * 64
                u0 = fall[a, lo : lo + 64, :].astype(jnp.float32)
                u1 = fall[a, TR + lo : TR + lo + 64, :].astype(jnp.float32)
                v0 = fall[e, lo : lo + 64, :].astype(jnp.float32)
                v1 = fall[e, TR + lo : TR + lo + 64, :].astype(jnp.float32)
                prod[0, 8 + lo : 72 + lo, :] = u0 * v0 + u1 * v1
                prod[1, 8 + lo : 72 + lo, :] = u1 * v0 - u0 * v1
                prod[2, 8 + lo : 72 + lo, :] = u0 * u0 + u1 * u1
                prod[3, 8 + lo : 72 + lo, :] = v0 * v0 + v1 * v1
            for f in range(4):
                for i in range(4):
                    lo = i * 64
                    s = prod[f, 5 + lo : 69 + lo, :]
                    for k in range(1, 7):
                        s = s + prod[f, 5 + lo + k : 69 + lo + k, :]
                    high = s.astype(jnp.bfloat16)
                    split[f, lo : lo + 64, 0:128] = high
                    split[f, lo : lo + 64, 128:256] = (s - high.astype(jnp.float32)).astype(jnp.bfloat16)
            for f in range(4):
                r = jnp.dot(split[f], bands[half], preferred_element_type=jnp.float32)
                acc[p, f] = r if half == 0 else acc[p, f] + r
            if half == 1:
                for i in range(8):
                    lo = i * 32
                    re, im = acc[p, 0, lo : lo + 32, :], acc[p, 1, lo : lo + 32, :]
                    pa, pe = acc[p, 2, lo : lo + 32, :], acc[p, 3, lo : lo + 32, :]
                    n = re * re + im * im
                    c = n * lax.rsqrt(jnp.maximum(n, 1e-30)) * lax.rsqrt(jnp.maximum(pa * pe, 1.0))
                    for side in range(2):
                        rows = pl.ds(side * NP * TR + lo * NP + p, 32, stride=NP)
                        result[rows, :] = c[:, side * 128 : (side + 1) * 128]

    @pl.loop(0, NQ + 4)
    def _(step):
        @pl.when(step < NQ)
        def _():
            q = step
            for k in (1, 3, 2):
                x_copy(q, k).wait_recv()
            own_copy(q).wait()
            begin(q, way_of(q), 4, 0)
            begin(q, -way_of(q), 3, 4)

        @pl.when((step >= 1) & (step < NQ + 1))
        def _():
            q = step - 1
            carry_on(q, way_of(q), 2, 2)
            carry_on(q, -way_of(q), 2, 5)

        for half, fall in enumerate((fall0, fall1)):
            first = half * 4

            @pl.when((step >= first + 2) & (step < first + 6))
            def _(fall=fall):
                finish(step - 2, fall)

            @pl.when((step >= first + 3) & (step < first + 7))
            def _(fall=fall):
                forward(step - 3, fall)

            @pl.when((step >= first + 4) & (step < first + 8))
            def _(fall=fall):
                arrive(step - 4, fall)

        @pl.when(step < NQ)
        def _():
            carry_on(step, way_of(step), 3, 1)

        @pl.when((step >= 1) & (step < NQ + 1))
        def _():
            q = step - 1
            carry_on(q, way_of(q), 1, 3)
            carry_on(q, -way_of(q), 1, 6)

        @pl.when(step == 8)
        def _():
            boxes(0, fall0)

    boxes(1, fall1)
    for side in range(2):
        out_copy(side).start()

    @pl.loop(0, NQ)
    def _(q):
        for k in (1, 3, 2):
            x_copy(q, k).wait_send()
        for n in range(7):
            z_copy(q, n, 1).wait_send()
        for k in (1, 2, 3):
            y_copy(fall0, q, k).wait_send()
        for k in range(NY):
            core_copy(fall0, q, k).wait_send()

    for side in range(2):
        out_copy(side).wait()


def main_call(z, koff, epochs):
    dma = pltpu.SemaphoreType.DMA
    field = pltpu.VMEM((32, 2 * TR, 128), jnp.bfloat16)
    return pl.pallas_call(
        main_kernel,
        out_shape=jax.ShapeDtypeStruct((TR, NP, 256), jnp.float32),
        in_specs=[
            pl.BlockSpec(memory_space=pl.ANY),
            pl.BlockSpec(memory_space=pltpu.VMEM),
            pl.BlockSpec(memory_space=pltpu.SMEM),
        ],
        out_specs=pl.BlockSpec(memory_space=pl.ANY),
        scratch_shapes=[
            pltpu.VMEM((NQ, NZ, NX * KP, 128), jnp.bfloat16),
            pltpu.VMEM((NX, NZ, 128), jnp.int32),
            pltpu.VMEM((NZ, 2 * TR, NX * KP), jnp.bfloat16),
            pltpu.VMEM((NQ, 7, MSG, 128), jnp.int16),
            pltpu.VMEM((NQ, 7, MSG, 128), jnp.int16),
            pltpu.VMEM((2 * TR, 128), jnp.float32),
            field,
            field,
            pltpu.VMEM((4, TR + 16, 128), jnp.float32),
            pltpu.VMEM((4, TR, 256), jnp.bfloat16),
            pltpu.VMEM((NP, 4, TR, 256), jnp.float32),
            pltpu.VMEM((2, 256, 256), jnp.bfloat16),
            pltpu.VMEM((2 * TR * NP, 128), jnp.float32),
            dma((NQ,)),
            dma((NQ, 3)), dma((NQ, 3)),
            dma((NQ, 7)), dma((NQ, 7)),
            dma((NQ, 3)), dma((NQ, 3)),
            dma((NQ, NY)), dma((NQ, NY)),
            dma((3,)), dma((3,)),
            dma((2,)),
        ],
        compiler_params=pltpu.CompilerParams(
            collective_id=0, has_side_effects=True, vmem_limit_bytes=48 * 2**20
        ),
        name="tiles_and_coherence",
    )(z, koff, epochs)


def local(radar_echoes, destination_panel, panel_line_shift, epoch_couples):
    z, koff = sort_blocks(radar_echoes, destination_panel[:, 0], panel_line_shift)
    z = z.reshape(NQ, NT, KS, 128)
    return main_call(z, koff, epoch_couples.T)


def solution(mesh):
    in_specs = (P("tile", None, "date", None, None), P("tile", None), P("tile"), P())
    out_specs = P("tile", "date", None)
    return jax.shard_map(local, mesh=mesh, in_specs=in_specs, out_specs=out_specs, check_vma=False)
```

```python
import functools

import jax
import jax.numpy as jnp
from jax import lax
from jax.experimental import pallas as pl
from jax.experimental.pallas import tpu as pltpu
from jax.sharding import PartitionSpec as P

NX, NZ, NY = 4, 8, 4
NT = NX * NZ
TR = 256
BR = 16
CAP = 3
BLK = 64
NQ = 8
KS = CAP * BR * 2
KP = 128
NP = 8
MSG = 2 * TR + 16
LEVELS = 32000.0
MESH = pl.DeviceIdType.MESH


def table_kernel(dest, shift, table, koff_ref, count):
    z = lax.rem(lax.axis_index("tile"), NZ)

    @pl.loop(0, NT)
    def _(t):
        count[t] = 0

    @pl.loop(0, 2 * NT * CAP)
    def _(s):
        table[s] = -1

    @pl.loop(0, BLK)
    def _(b):
        t = dest[b]
        k = count[t]
        count[t] = k + 1
        column, off = (t // NZ) * NZ, lax.rem(t, NZ) - z
        table[(column + ((off + 2) & 7)) * CAP + k] = b
        table[(NT + column + ((2 - off) & 7)) * CAP + k] = b

    lane = lax.broadcasted_iota(jnp.int32, (1, 128), 1)
    slot = lane >> 5
    inside = ((lane & 31) >> 1) + TR * (lane & 1)

    @pl.loop(0, 2 * NT)
    def _(t):
        value = jnp.full((1, 128), -1, jnp.int32)
        for k in range(CAP):
            b = table[t * CAP + k]
            start = jnp.where(b >= 0, shift[jnp.maximum(b, 0)], -4096)
            value = jnp.where(slot == k, start + inside, value)
        koff_ref[t] = value


def block_tables(dest, shift):
    smem = pl.BlockSpec(memory_space=pltpu.SMEM)
    return pl.pallas_call(
        table_kernel,
        out_shape=(
            jax.ShapeDtypeStruct((2 * NT * CAP,), jnp.int32),
            jax.ShapeDtypeStruct((2 * NT, 1, 128), jnp.int32),
        ),
        in_specs=[smem, smem],
        out_specs=(smem, pl.BlockSpec(memory_space=pltpu.VMEM)),
        scratch_shapes=[pltpu.SMEM((NT,), jnp.int32)],
        name="block_tables",
    )(dest, shift)


def encode(total, out, rows):
    top = jnp.maximum(jnp.max(rows, axis=0, keepdims=True), 1e-30)
    power = jnp.clip(jnp.ceil(jnp.log2(top)), -100.0, 100.0)
    out[2 * TR :, :] = jnp.broadcast_to(power, (16, 128)).astype(jnp.int32).astype(jnp.int16)
    scale = jnp.exp2(-power)
    for i in range(4):
        v = total[i * 128 : (i + 1) * 128, :]
        y = jnp.abs(v) * scale
        y = y * lax.rsqrt(jnp.maximum(y, 1e-30))
        y = y * lax.rsqrt(jnp.maximum(y, 1e-15))
        m = (y * LEVELS + 0.5).astype(jnp.int32)
        out[i * 128 : (i + 1) * 128, :] = jnp.where(v < 0, -m, m).astype(jnp.int16)


def scale_of(msg):
    power = msg[2 * TR :, :].astype(jnp.int32).astype(jnp.float32)
    return jnp.exp2(power[0:1, :])


def decode(msg, scale, i):
    f = msg[i * 128 : (i + 1) * 128, :].astype(jnp.int32).astype(jnp.float32) * (1.0 / LEVELS)
    f = f * jnp.abs(f)
    f = f * jnp.abs(f)
    return f * scale


def main_kernel(
    table, koff_ref, ep_ref, x_ref, out_ref,
    held, zb, got, kof, place, sent, came, total, fall0, fall1, prod, split, acc, bands, result,
    in_sem, own_sem, xs_sem, xr_sem, zs_sem, zr_sem, ys_sem, yr_sem, cs_sem, cr_sem, ks_sem, kr_sem, out_sem,
):
    d = lax.axis_index("date")
    t = lax.axis_index("tile")
    y, core = d // 2, lax.rem(d, 2)
    x, z = t // NZ, lax.rem(t, NZ)
    partner = (y * 2 + 1 - core, t)

    def at(dx, dz):
        return (d, lax.rem(x + dx, NX) * NZ + lax.rem(z + dz + NZ, NZ))

    def at_y(k):
        return (lax.rem(y + k, NY) * 2 + core, t)

    def load(q):
        half, date = divmod(q, 4)
        return pltpu.make_async_copy(
            x_ref.at[:, :, date, :, pl.ds(half * 128, 128)], held.at[pl.ds(q * BLK, BLK)], in_sem.at[q]
        )

    for q in range(NQ):
        load(q).start()

    @pl.loop(0, NQ)
    def _(q):
        for j in range(NZ):
            for s in range(NX):
                got[q, j, s * KP + KS : (s + 1) * KP, :] = jnp.zeros((KP - KS, 128), jnp.bfloat16)

    barrier = pltpu.get_barrier_semaphore()
    peers = [at(1, 0), at(2, 0), at(3, 0), at_y(1), at_y(2), at_y(3), partner]
    peers += [at(k, way) for k in range(NX) for way in (1, -1)]
    for peer in peers:
        pl.semaphore_signal(barrier, 1, device_id=peer, device_id_type=MESH)
    pl.semaphore_wait(barrier, len(peers))

    def remote(src, dst, ssem, rsem, dev):
        return pltpu.make_async_remote_copy(
            src_ref=src, dst_ref=dst, send_sem=ssem, recv_sem=rsem, device_id=dev, device_id_type=MESH
        )

    def way_of(q):
        return 1 - 2 * lax.rem(q, 2)

    def koff_copies(par):
        copies = []
        for k in (1, 3, 2):
            there = lax.rem(x + k, NX)
            copies.append(remote(
                koff_ref.at[pl.ds(par * NT + there * NZ, 6)], kof.at[par, x, pl.ds(0, 6)],
                ks_sem.at[par, k], kr_sem.at[par, k], at(k, 0),
            ))
        for m, way in ((6, 1 - 2 * par), (7, 2 * par - 1)):
            for k in range(NX):
                there, n = lax.rem(x + k, NX), 4 * (m - 5) + k
                copies.append(remote(
                    koff_ref.at[par * NT + there * NZ + m], kof.at[par, x, m],
                    ks_sem.at[par, n], kr_sem.at[par, n], at(k, way),
                ))
        return copies

    def x_copies(q):
        rows = pl.ds(pl.multiple_of(x * KP, KP), KS)
        copies = []
        for m, way in ((6, way_of(q)), (7, -way_of(q))):
            for k in range(NX):
                there, n = lax.rem(x + k, NX), 4 * (m - 5) + k
                copies.append(remote(
                    zb.at[q, there * NZ + m], got.at[q, m, rows],
                    xs_sem.at[q, n], xr_sem.at[q, n], at(k, way),
                ))
        for k in (1, 3, 2):
            there = lax.rem(x + k, NX)
            copies.append(remote(
                zb.at[q, pl.ds(there * NZ, 6)], got.at[q, pl.ds(0, 6), rows],
                xs_sem.at[q, k], xr_sem.at[q, k], at(k, 0),
            ))
        return copies

    def own_copy(q):
        return pltpu.make_async_copy(
            zb.at[q, pl.ds(x * NZ, 6)], got.at[q, pl.ds(0, 6), pl.ds(pl.multiple_of(x * KP, KP), KS)],
            own_sem.at[q],
        )

    for par in range(2):
        for copy in koff_copies(par):
            copy.start()
    for q in range(NQ):
        load(q).wait()

    blocks = held.reshape(NQ * BLK, 2 * BR, 128)

    def send_blocks(q):
        par = lax.rem(q, 2)

        @pl.loop(0, NT)
        def _(i):
            for k in range(CAP):
                b = table[(par * NT + i) * CAP + k]
                v = blocks[q * BLK + jnp.maximum(b, 0)]
                zb[q, i, k * 32 : (k + 1) * 32, :] = jnp.where(b >= 0, v, jnp.zeros_like(v))

        for copy in x_copies(q):
            copy.start()
        own_copy(q).start()

    def build(par):
        kof[par, x, 0:6] = koff_ref[pl.ds(par * NT + x * NZ, 6)]
        for copy in koff_copies(par):
            copy.wait()

        @pl.loop(0, NZ)
        def _(j):
            for s in range(NX):
                goal = kof[par, s, j]
                for i in range(4):
                    row = lax.broadcasted_iota(jnp.int32, (128, 128), 0) + i * 128
                    hit = jnp.where(row == goal, 1.0, 0.0).astype(jnp.bfloat16)
                    place[par, j, i * 128 : (i + 1) * 128, s * 128 : (s + 1) * 128] = hit

    @pl.loop(0, 3)
    def _(q):
        send_blocks(q)

    build(0)
    build(1)
    for half in range(2):
        i = lax.broadcasted_iota(jnp.int32, (256, 256), 0)
        j = lax.broadcasted_iota(jnp.int32, (256, 256), 1)
        near = jnp.abs((i & 127) + half * 128 - j) <= 7
        bands[half] = jnp.where(near, 1.0, 0.0).astype(jnp.bfloat16)
    prod[...] = jnp.zeros_like(prod)

    def part(q, j, i):
        return jnp.dot(
            place[lax.rem(q, 2), j, i * 128 : (i + 1) * 128, :], got[q, j],
            preferred_element_type=jnp.float32,
        )

    def z_copy(q, n, way):
        return remote(sent.at[q, n], came.at[q, n], zs_sem.at[q, n], zr_sem.at[q, n], at(0, way))

    def begin(q, way, j, n):
        top = jnp.zeros((8, 128), jnp.float32)
        for i in range(4):
            v = part(q, j[0], i) + part(q, j[1], i)
            total[i * 128 : (i + 1) * 128, :] = v
            top = jnp.maximum(top, jnp.max(jnp.abs(v).reshape(16, 8, 128), axis=0))
        encode(total, sent.at[q, n], top)
        z_copy(q, n, way).start()

    def carry_on(q, way, j, n):
        z_copy(q, n - 1, way).wait_recv()
        msg = came.at[q, n - 1]
        scale = scale_of(msg)
        top = jnp.zeros((8, 128), jnp.float32)
        for i in range(4):
            v = part(q, j, i) + decode(msg, scale, i)
            total[i * 128 : (i + 1) * 128, :] = v
            top = jnp.maximum(top, jnp.max(jnp.abs(v).reshape(16, 8, 128), axis=0))
        encode(total, sent.at[q, n], top)
        z_copy(q, n, way).start()

    def y_copy(fall, q, k):
        mine = fall.at[d * 4 + lax.rem(q, 4)]
        return remote(mine, mine, ys_sem.at[q, k - 1], yr_sem.at[q, k - 1], at_y(k))

    def core_copy(fall, q, k):
        from_d = lax.rem(y - k + NY, NY) * 2 + core
        field = fall.at[from_d * 4 + lax.rem(q, 4)]
        return remote(field, field, cs_sem.at[q, k], cr_sem.at[q, k], partner)

    def finish(q, fall):
        way = way_of(q)
        z_copy(q, 2, way).wait_recv()
        z_copy(q, 4, -way).wait_recv()
        one, two = came.at[q, 2], came.at[q, 4]
        s1, s2 = scale_of(one), scale_of(two)
        for i in range(4):
            v = part(q, 2, i) + (decode(one, s1, i) + decode(two, s2, i))
            fall[d * 4 + lax.rem(q, 4), i * 128 : (i + 1) * 128, :] = v.astype(jnp.bfloat16)
        for k in (1, 3, 2):
            y_copy(fall, q, k).start()
        core_copy(fall, q, 0).start()

    def forward(q, fall):
        for k in (1, 3, 2):
            y_copy(fall, q, k).wait_recv()
            core_copy(fall, q, k).start()

    def arrive(q, fall):
        for k in range(NY):
            core_copy(fall, q, k).wait_recv()

    def out_copy(side):
        return pltpu.make_async_copy(
            result.reshape(2, TR, NP, 128).at[side],
            out_ref.at[:, :, pl.ds(side * 128, 128)],
            out_sem.at[side],
        )

    def boxes(half, fall, first, number):
        @pl.loop(first, first + number)
        def _(p):
            a = ep_ref[0, d * NP + p]
            e = ep_ref[1, d * NP + p]
            for i in range(4):
                lo = i * 64
                u0 = fall[a, lo : lo + 64, :].astype(jnp.float32)
                u1 = fall[a, TR + lo : TR + lo + 64, :].astype(jnp.float32)
                v0 = fall[e, lo : lo + 64, :].astype(jnp.float32)
                v1 = fall[e, TR + lo : TR + lo + 64, :].astype(jnp.float32)
                prod[0, 8 + lo : 72 + lo, :] = u0 * v0 + u1 * v1
                prod[1, 8 + lo : 72 + lo, :] = u1 * v0 - u0 * v1
                prod[2, 8 + lo : 72 + lo, :] = u0 * u0 + u1 * u1
                prod[3, 8 + lo : 72 + lo, :] = v0 * v0 + v1 * v1
            for f in range(4):
                for i in range(4):
                    lo = i * 64
                    s = prod[f, 5 + lo : 69 + lo, :]
                    for k in range(1, 7):
                        s = s + prod[f, 5 + lo + k : 69 + lo + k, :]
                    high = s.astype(jnp.bfloat16)
                    split[f, lo : lo + 64, 0:128] = high
                    split[f, lo : lo + 64, 128:256] = (s - high.astype(jnp.float32)).astype(jnp.bfloat16)
            for f in range(4):
                r = jnp.dot(split[f], bands[half], preferred_element_type=jnp.float32)
                acc[p, f] = r if half == 0 else acc[p, f] + r
            if half == 1:
                for i in range(8):
                    lo = i * 32
                    re, im = acc[p, 0, lo : lo + 32, :], acc[p, 1, lo : lo + 32, :]
                    pa, pe = acc[p, 2, lo : lo + 32, :], acc[p, 3, lo : lo + 32, :]
                    n = re * re + im * im
                    c = n * lax.rsqrt(jnp.maximum(n, 1e-30)) * lax.rsqrt(jnp.maximum(pa * pe, 1.0))
                    for side in range(2):
                        rows = pl.ds(side * NP * TR + lo * NP + p, 32, stride=NP)
                        result[rows, :] = c[:, side * 128 : (side + 1) * 128]

    @pl.loop(0, NQ + 3)
    def _(step):
        @pl.when(step < NQ)
        def _():
            q = step
            way = way_of(q)
            for copy in x_copies(q):
                copy.wait_recv()
            own_copy(q).wait()
            begin(q, way, (5, 6), 0)
            begin(q, -way, (0, 7), 3)

        @pl.when((step >= 1) & (step < NQ + 1))
        def _():
            carry_on(step - 1, way_of(step - 1), 3, 2)

        @pl.when(step + 3 < NQ)
        def _():
            send_blocks(step + 3)

        for half, fall in enumerate((fall0, fall1)):
            first = half * 4

            @pl.when((step >= first + 2) & (step < first + 6))
            def _(fall=fall):
                forward(step - 2, fall)

            @pl.when((step >= first + 3) & (step < first + 7))
            def _(fall=fall):
                arrive(step - 3, fall)

        @pl.when(step < NQ)
        def _():
            way = way_of(step)
            carry_on(step, way, 4, 1)
            carry_on(step, -way, 1, 4)

        for half, fall in enumerate((fall0, fall1)):
            first = half * 4

            @pl.when((step >= first + 1) & (step < first + 5))
            def _(fall=fall):
                finish(step - 1, fall)

        @pl.when((step >= 6) & (step < 10))
        def _():
            boxes(0, fall0, (step - 6) * 2, 2)

    boxes(1, fall1, 0, NP)
    for side in range(2):
        out_copy(side).start()

    @pl.loop(0, NQ)
    def _(q):
        for copy in x_copies(q):
            copy.wait_send()
        for n in range(5):
            z_copy(q, n, 1).wait_send()
        for k in (1, 2, 3):
            y_copy(fall0, q, k).wait_send()
        for k in range(NY):
            core_copy(fall0, q, k).wait_send()

    for side in range(2):
        out_copy(side).wait()


def main_call(table, koff, epochs, x):
    dma = pltpu.SemaphoreType.DMA
    field = pltpu.VMEM((32, 2 * TR, 128), jnp.bfloat16)
    smem = pl.BlockSpec(memory_space=pltpu.SMEM)
    return pl.pallas_call(
        main_kernel,
        out_shape=jax.ShapeDtypeStruct((TR, NP, 256), jnp.float32),
        in_specs=[smem, pl.BlockSpec(memory_space=pltpu.VMEM), smem, pl.BlockSpec(memory_space=pl.ANY)],
        out_specs=pl.BlockSpec(memory_space=pl.ANY),
        scratch_shapes=[
            pltpu.VMEM((NQ * BLK, BR, 2, 128), jnp.bfloat16),
            pltpu.VMEM((NQ, NT, KS, 128), jnp.bfloat16),
            pltpu.VMEM((NQ, NZ, NX * KP, 128), jnp.bfloat16),
            pltpu.VMEM((2, NX, NZ, 1, 128), jnp.int32),
            pltpu.VMEM((2, NZ, 2 * TR, NX * KP), jnp.bfloat16),
            pltpu.VMEM((NQ, 5, MSG, 128), jnp.int16),
            pltpu.VMEM((NQ, 5, MSG, 128), jnp.int16),
            pltpu.VMEM((2 * TR, 128), jnp.float32),
            field,
            field,
            pltpu.VMEM((4, TR + 16, 128), jnp.float32),
            pltpu.VMEM((4, TR, 256), jnp.bfloat16),
            pltpu.VMEM((NP, 4, TR, 256), jnp.float32),
            pltpu.VMEM((2, 256, 256), jnp.bfloat16),
            pltpu.VMEM((2 * TR * NP, 128), jnp.float32),
            dma((NQ,)), dma((NQ,)),
            dma((NQ, 12)), dma((NQ, 12)),
            dma((NQ, 5)), dma((NQ, 5)),
            dma((NQ, 3)), dma((NQ, 3)),
            dma((NQ, NY)), dma((NQ, NY)),
            dma((2, 12)), dma((2, 12)),
            dma((2,)),
        ],
        compiler_params=pltpu.CompilerParams(
            collective_id=0, has_side_effects=True, vmem_limit_bytes=58 * 2**20
        ),
        name="tiles_and_coherence",
    )(table, koff, epochs, x)


def local(radar_echoes, destination_panel, panel_line_shift, epoch_couples):
    table, koff = block_tables(destination_panel[:, 0], panel_line_shift)
    return main_call(table, koff, epoch_couples.T, radar_echoes)


def solution(mesh):
    in_specs = (P("tile", None, "date", None, None), P("tile", None), P("tile"), P())
    out_specs = P("tile", "date", None)
    return jax.shard_map(local, mesh=mesh, in_specs=in_specs, out_specs=out_specs, check_vma=False)
```

```python
import functools

import jax
import jax.numpy as jnp
from jax import lax
from jax.experimental import pallas as pl
from jax.experimental.pallas import tpu as pltpu
from jax.sharding import PartitionSpec as P

NX, NZ, NY = 4, 8, 4
NT = NX * NZ
TR = 256
BR = 16
CAP = 3
BLK = 64
NQ = 8
KS = CAP * BR * 2
KP = 128
NP = 8
MSG = 2 * TR + 16
PIECE = TR + 16
SLOT = (5, 4, 2, 1, 6, 7, 0, 3)
LEVELS = 32000.0
MESH = pl.DeviceIdType.MESH


def power_of(top):
    return jnp.clip(jnp.ceil(jnp.log2(jnp.maximum(top, 1e-30))), -100.0, 100.0)


def encode(v, scale):
    y = jnp.abs(v) * scale
    y = y * lax.rsqrt(jnp.maximum(y, 1e-30))
    y = y * lax.rsqrt(jnp.maximum(y, 1e-15))
    m = (y * LEVELS + 0.5).astype(jnp.int32)
    return jnp.where(v < 0, -m, m).astype(jnp.int16)


def decode(code, scale):
    f = code.astype(jnp.int32).astype(jnp.float32) * (1.0 / LEVELS)
    f = f * jnp.abs(f)
    f = f * jnp.abs(f)
    return f * scale


def scale_of(power):
    return jnp.exp2(power.astype(jnp.int32).astype(jnp.float32)[0:1, :])


def main_kernel(
    dest_ref, shift_ref, ep_ref, x_ref, out_ref,
    table, listed, koff_ref, held, zb, got, kof, place, sent, came, total, fall0, fall1, prod, split, keep, bands, result,
    in_sem, own_sem, xs_sem, xr_sem, zs_sem, zr_sem, ys_sem, yr_sem, cs_sem, cr_sem, ks_sem, kr_sem, out_sem, table_sem,
):
    d = lax.axis_index("date")
    t = lax.axis_index("tile")
    y, core = d // 2, lax.rem(d, 2)
    x, z = t // NZ, lax.rem(t, NZ)
    partner = (y * 2 + 1 - core, t)

    def at(dx, dz):
        return (d, lax.rem(x + dx, NX) * NZ + lax.rem(z + dz + NZ, NZ))

    def at_y(k):
        return (lax.rem(y + k, NY) * 2 + core, t)

    def load(q):
        half, date = divmod(q, 4)
        return pltpu.make_async_copy(
            x_ref.at[:, :, date, :, pl.ds(half * 128, 128)], held.at[pl.ds(q * BLK, BLK)], in_sem.at[q]
        )

    for q in range(NQ):
        load(q).start()

    r = lax.broadcasted_iota(jnp.int32, (BLK, BLK), 0)
    c = lax.broadcasted_iota(jnp.int32, (BLK, BLK), 1)
    dest = dest_ref[...]
    along = jnp.broadcast_to(dest, (BLK, BLK)).astype(jnp.float32)
    shifts = jnp.broadcast_to(shift_ref[...], (BLK, BLK)).astype(jnp.float32)
    down = jnp.sum(jnp.where(r == c, along, 0.0), axis=1, keepdims=True)
    shift = jnp.sum(jnp.where(r == c, shifts, 0.0), axis=1, keepdims=True)
    rank = jnp.sum(jnp.where((down == along) & (c < r), 1.0, 0.0), axis=1, keepdims=True)
    lane = lax.broadcasted_iota(jnp.int32, (BLK, 128), 1)
    number = lax.broadcasted_iota(jnp.int32, (BLK, 128), 0)
    chosen = (lane >> 5).astype(jnp.float32) == rank
    off = (dest & (NZ - 1)) - z
    hit = jnp.zeros((BLK, BLK), jnp.float32)
    for par in range(2):
        turn = (off if par == 0 else -off) & (NZ - 1)
        index = par * NT + (dest - (dest & (NZ - 1)))
        for n, slot in enumerate(SLOT):
            index = index + jnp.where(turn == n, slot, 0)
        hit = hit + jnp.where(r == index, 1.0, 0.0)
    hit = hit.astype(jnp.bfloat16)
    first = jnp.where(chosen, (number + 1).astype(jnp.float32), 0.0).astype(jnp.bfloat16)
    second = jnp.where(chosen, shift + 1.0, 0.0).astype(jnp.bfloat16)
    listed[...] = jnp.dot(hit, first, preferred_element_type=jnp.float32).astype(jnp.int32) - 1
    start = jnp.dot(hit, second, preferred_element_type=jnp.float32).astype(jnp.int32)
    goals = jnp.where(start > 0, start - 1 + ((lane & 31) >> 1) + TR * (lane & 1), -1)
    for n in range(2 * NT):
        koff_ref[n] = goals[n : n + 1, :]
    table_copy = pltpu.make_async_copy(listed, table, table_sem)
    table_copy.start()

    @pl.loop(0, NQ)
    def _(q):
        for j in range(NZ):
            for s in range(NX):
                got[q, j, s * KP + KS : (s + 1) * KP, :] = jnp.zeros((KP - KS, 128), jnp.bfloat16)

    barrier = pltpu.get_barrier_semaphore()
    peers = [at(1, 0), at(2, 0), at(3, 0), at_y(1), at_y(2), at_y(3), partner]
    peers += [at(k, way) for k in range(NX) for way in (1, -1)]
    for peer in peers:
        pl.semaphore_signal(barrier, 1, device_id=peer, device_id_type=MESH)
    pl.semaphore_wait(barrier, len(peers))

    def remote(src, dst, ssem, rsem, dev):
        return pltpu.make_async_remote_copy(
            src_ref=src, dst_ref=dst, send_sem=ssem, recv_sem=rsem, device_id=dev, device_id_type=MESH
        )

    def way_of(q):
        return 1 - 2 * lax.rem(q, 2)

    def koff_copies(par):
        copies = []
        for k in (1, 3, 2):
            there = lax.rem(x + k, NX)
            copies.append(remote(
                koff_ref.at[pl.ds(par * NT + there * NZ, 6)], kof.at[par, x, pl.ds(0, 6)],
                ks_sem.at[par, k], kr_sem.at[par, k], at(k, 0),
            ))
        for m, way in ((6, 1 - 2 * par), (7, 2 * par - 1)):
            for k in range(NX):
                there, n = lax.rem(x + k, NX), 4 * (m - 5) + k
                copies.append(remote(
                    koff_ref.at[par * NT + there * NZ + m], kof.at[par, x, m],
                    ks_sem.at[par, n], kr_sem.at[par, n], at(k, way),
                ))
        return copies

    def x_group(q, g):
        rows = pl.ds(pl.multiple_of(x * KP, KP), KS)
        copies = []
        if g > 0:
            for k in (1, 3, 2):
                first, n = lax.rem(x + k, NX) * NZ + 2 * g - 2, 8 + 4 * g + k
                copies.append(remote(
                    zb.at[q, pl.ds(first, 2)], got.at[q, pl.ds(2 * g - 2, 2), rows],
                    xs_sem.at[q, n], xr_sem.at[q, n], at(k, 0),
                ))
            return copies
        for m, way in ((6, way_of(q)), (7, -way_of(q))):
            for k in range(NX):
                there, n = lax.rem(x + k, NX), 4 * (m - 5) + k
                copies.append(remote(
                    zb.at[q, there * NZ + m], got.at[q, m, rows],
                    xs_sem.at[q, n], xr_sem.at[q, n], at(k, way),
                ))
        return copies

    def own_copy(q):
        return pltpu.make_async_copy(
            zb.at[q, pl.ds(x * NZ, 6)], got.at[q, pl.ds(0, 6), pl.ds(pl.multiple_of(x * KP, KP), KS)],
            own_sem.at[q],
        )

    for par in range(2):
        for copy in koff_copies(par):
            copy.start()
    for q in range(NQ):
        load(q).wait()
    table_copy.wait()

    blocks = held.reshape(NQ * BLK, 2 * BR, 128)

    def send_blocks(q):
        par = lax.rem(q, 2)

        @pl.loop(0, NT)
        def _(i):
            for k in range(CAP):
                b = table[par * NT + i, k * 32]
                v = blocks[q * BLK + jnp.minimum(jnp.maximum(b, 0), BLK - 1)]
                zb[q, i, k * 32 : (k + 1) * 32, :] = jnp.where(b >= 0, v, jnp.zeros_like(v))

        for g in range(4):
            for copy in x_group(q, g):
                copy.start()
        own_copy(q).start()

    def build(par):
        kof[par, x, 0:6] = koff_ref[pl.ds(par * NT + x * NZ, 6)]
        for copy in koff_copies(par):
            copy.wait()

        @pl.loop(0, NZ)
        def _(j):
            for s in range(NX):
                goal = kof[par, s, j]
                for i in range(4):
                    row = lax.broadcasted_iota(jnp.int32, (128, 128), 0) + i * 128
                    hit = jnp.where(row == goal, 1.0, 0.0).astype(jnp.bfloat16)
                    place[par, j, i * 128 : (i + 1) * 128, s * 128 : (s + 1) * 128] = hit

    @pl.loop(0, 3)
    def _(q):
        send_blocks(q)

    build(0)
    build(1)
    for half in range(2):
        i = lax.broadcasted_iota(jnp.int32, (256, 256), 0)
        j = lax.broadcasted_iota(jnp.int32, (256, 256), 1)
        near = jnp.abs((i & 127) + half * 128 - j) <= 7
        bands[half] = jnp.where(near, 1.0, 0.0).astype(jnp.bfloat16)
    prod[...] = jnp.zeros_like(prod)

    def part(q, j, i):
        return jnp.dot(
            place[lax.rem(q, 2), j, i * 128 : (i + 1) * 128, :], got[q, j],
            preferred_element_type=jnp.float32,
        )

    def z_copy(q, n, h, way):
        piece = pl.ds(h * PIECE, PIECE if h == 0 else TR)
        return remote(
            sent.at[q, n, piece], came.at[q, n, piece], zs_sem.at[q, 2 * n + h], zr_sem.at[q, 2 * n + h], at(0, way)
        )

    def own_part(q, slots, at_total):
        top = jnp.zeros((8, 128), jnp.float32)
        for i in range(4):
            v = part(q, slots[0], i)
            for slot in slots[1:]:
                v = v + part(q, slot, i)
            total[at_total, i * 128 : (i + 1) * 128, :] = v
            top = jnp.maximum(top, jnp.max(jnp.abs(v).reshape(16, 8, 128), axis=0))
        return jnp.max(top, axis=0, keepdims=True)

    def hop(q, units):
        tops = [own_part(q, slots, u) for u, (_, slots, _, _) in enumerate(units)]
        scales = [None] * len(units)
        for h in range(2):
            for u, (way, _, taken, n) in enumerate(units):
                if taken is not None:
                    z_copy(q, taken, h, way).wait_recv()
                if h == 0:
                    arrived = None
                    if taken is not None:
                        arrived = scale_of(came[q, taken, 2 * 128 : PIECE, :])
                        tops[u] = tops[u] + arrived
                    power = power_of(tops[u])
                    sent[q, n, 2 * 128 : PIECE, :] = (
                        jnp.broadcast_to(power, (16, 128)).astype(jnp.int32).astype(jnp.int16)
                    )
                    scales[u] = (arrived, jnp.exp2(-power))
                arrived, scale = scales[u]
                for part_no in range(2):
                    i = part_no * 2 + h
                    rows = slice(h * PIECE + part_no * 128, h * PIECE + part_no * 128 + 128)
                    v = total[u, i * 128 : (i + 1) * 128, :]
                    if taken is not None:
                        v = v + decode(came[q, taken, rows, :], arrived)
                    sent[q, n, rows, :] = encode(v, scale)
                z_copy(q, n, h, way).start()

    def y_copy(fall, q, k, h):
        mine = fall.at[d * 4 + lax.rem(q, 4), :, pl.ds(h * 128, 128)]
        n = 2 * k - 2 + h
        return remote(mine, mine, ys_sem.at[q, n], yr_sem.at[q, n], at_y(k))

    def core_copy(fall, q, k, h):
        from_d = lax.rem(y - k + NY, NY) * 2 + core
        field = fall.at[from_d * 4 + lax.rem(q, 4), :, pl.ds(h * 128, 128)]
        return remote(field, field, cs_sem.at[q, 2 * k + h], cr_sem.at[q, 2 * k + h], partner)

    def finish(q, fall):
        way = way_of(q)
        own_part(q, (5,), 0)
        scales = [None, None]
        for h in range(2):
            for u, (n, w) in enumerate(((2, way), (4, -way))):
                z_copy(q, n, h, w).wait_recv()
                if h == 0:
                    scales[u] = scale_of(came[q, n, 2 * 128 : PIECE, :])
            for part_no in range(2):
                i = part_no * 2 + h
                rows = slice(h * PIECE + part_no * 128, h * PIECE + part_no * 128 + 128)
                v = total[0, i * 128 : (i + 1) * 128, :]
                v = v + (decode(came[q, 2, rows, :], scales[0]) + decode(came[q, 4, rows, :], scales[1]))
                fall[d * 4 + lax.rem(q, 4), part_no, h * 128 : (h + 1) * 128, :] = v.astype(jnp.bfloat16)
            for k in (1, 3, 2):
                y_copy(fall, q, k, h).start()
            core_copy(fall, q, 0, h).start()

    def forward(q, fall):
        for h in range(2):
            for k in (1, 3, 2):
                y_copy(fall, q, k, h).wait_recv()
                core_copy(fall, q, k, h).start()

    def arrive(q, fall):
        for h in range(2):
            for k in range(NY):
                core_copy(fall, q, k, h).wait_recv()

    def out_copy(side):
        return pltpu.make_async_copy(
            result.reshape(2, TR, NP, 128).at[side],
            out_ref.at[:, :, pl.ds(side * 128, 128)],
            out_sem.at[side],
        )

    def boxes(half, fall, first, number):
        @pl.loop(first, first + number)
        def _(p):
            a = ep_ref[0, d * NP + p]
            e = ep_ref[1, d * NP + p]
            for i in range(4):
                lo = i * 64
                u0 = fall[a, 0, lo : lo + 64, :].astype(jnp.float32)
                u1 = fall[a, 1, lo : lo + 64, :].astype(jnp.float32)
                v0 = fall[e, 0, lo : lo + 64, :].astype(jnp.float32)
                v1 = fall[e, 1, lo : lo + 64, :].astype(jnp.float32)
                prod[0, 8 + lo : 72 + lo, :] = u0 * v0 + u1 * v1
                prod[1, 8 + lo : 72 + lo, :] = u1 * v0 - u0 * v1
                prod[2, 8 + lo : 72 + lo, :] = u0 * u0 + u1 * u1
                prod[3, 8 + lo : 72 + lo, :] = v0 * v0 + v1 * v1
            for f in range(4):
                for i in range(4):
                    lo = i * 64
                    s = prod[f, 5 + lo : 69 + lo, :]
                    for k in range(1, 7):
                        s = s + prod[f, 5 + lo + k : 69 + lo + k, :]
                    high = s.astype(jnp.bfloat16)
                    low = (s - high.astype(jnp.float32)).astype(jnp.bfloat16)
                    if half == 0:
                        keep[p, f, lo : lo + 64, 0:128] = high
                        keep[p, f, lo : lo + 64, 128:256] = low
                    else:
                        split[f, lo : lo + 64, 0:128] = high
                        split[f, lo : lo + 64, 128:256] = low
            if half == 1:
                for i in range(4):
                    lo = i * 64
                    re, im, pa, pe = [
                        jnp.dot(keep[p, f, lo : lo + 64, :], bands[0], preferred_element_type=jnp.float32)
                        + jnp.dot(split[f, lo : lo + 64, :], bands[1], preferred_element_type=jnp.float32)
                        for f in range(4)
                    ]
                    n = re * re + im * im
                    c = n * lax.rsqrt(jnp.maximum(n, 1e-30)) * lax.rsqrt(jnp.maximum(pa * pe, 1.0))
                    for side in range(2):
                        rows = pl.ds(side * NP * TR + lo * NP + p, 64, stride=NP)
                        result[rows, :] = c[:, side * 128 : (side + 1) * 128]

    @pl.loop(0, NQ + 3)
    def _(step):
        @pl.when(step < NQ)
        def _():
            for copy in x_group(step, 0) + x_group(step, 1):
                copy.wait_recv()
            own_copy(step).wait()
            hop(step, ((way_of(step), (1, 6), None, 0), (-way_of(step), (0, 7), None, 3)))

        @pl.when((step >= 1) & (step < NQ + 1))
        def _():
            for copy in x_group(step - 1, 3):
                copy.wait_recv()
            hop(step - 1, ((way_of(step - 1), (4,), 1, 2),))

        @pl.when(step + 3 < NQ)
        def _():
            send_blocks(step + 3)

        for half, fall in enumerate((fall0, fall1)):
            first = half * 4

            @pl.when((step >= first + 2) & (step < first + 6))
            def _(fall=fall):
                forward(step - 2, fall)

            @pl.when((step >= first + 3) & (step < first + 7))
            def _(fall=fall):
                arrive(step - 3, fall)

        @pl.when(step < NQ)
        def _():
            for copy in x_group(step, 2):
                copy.wait_recv()
            hop(step, ((way_of(step), (2,), 0, 1), (-way_of(step), (3,), 3, 4)))

        for half, fall in enumerate((fall0, fall1)):
            first = half * 4

            @pl.when((step >= first + 1) & (step < first + 5))
            def _(fall=fall):
                finish(step - 1, fall)

        @pl.when((step >= 6) & (step < 10))
        def _():
            boxes(0, fall0, (step - 6) * 2, 2)

    boxes(1, fall1, 0, NP)
    for side in range(2):
        out_copy(side).start()

    @pl.loop(0, NQ)
    def _(q):
        for g in range(4):
            for copy in x_group(q, g):
                copy.wait_send()
        for h in range(2):
            for n in range(5):
                z_copy(q, n, h, 1).wait_send()
            for k in (1, 2, 3):
                y_copy(fall0, q, k, h).wait_send()
            for k in range(NY):
                core_copy(fall0, q, k, h).wait_send()

    for side in range(2):
        out_copy(side).wait()


def main_call(dest, shift, epochs, x):
    dma = pltpu.SemaphoreType.DMA
    field = pltpu.VMEM((32, 2, TR, 128), jnp.bfloat16)
    vmem = pl.BlockSpec(memory_space=pltpu.VMEM)
    return pl.pallas_call(
        main_kernel,
        out_shape=jax.ShapeDtypeStruct((TR, NP, 256), jnp.float32),
        in_specs=[vmem, vmem, pl.BlockSpec(memory_space=pltpu.SMEM), pl.BlockSpec(memory_space=pl.ANY)],
        out_specs=pl.BlockSpec(memory_space=pl.ANY),
        scratch_shapes=[
            pltpu.SMEM((2 * NT, 128), jnp.int32),
            pltpu.VMEM((2 * NT, 128), jnp.int32),
            pltpu.VMEM((2 * NT, 1, 128), jnp.int32),
            pltpu.VMEM((NQ * BLK, BR, 2, 128), jnp.bfloat16),
            pltpu.VMEM((NQ, NT, KS, 128), jnp.bfloat16),
            pltpu.VMEM((NQ, NZ, NX * KP, 128), jnp.bfloat16),
            pltpu.VMEM((2, NX, NZ, 1, 128), jnp.int32),
            pltpu.VMEM((2, NZ, 2 * TR, NX * KP), jnp.bfloat16),
            pltpu.VMEM((NQ, 5, MSG, 128), jnp.int16),
            pltpu.VMEM((NQ, 5, MSG, 128), jnp.int16),
            pltpu.VMEM((2, 2 * TR, 128), jnp.float32),
            field,
            field,
            pltpu.VMEM((4, TR + 16, 128), jnp.float32),
            pltpu.VMEM((4, TR, 256), jnp.bfloat16),
            pltpu.VMEM((NP, 4, TR, 256), jnp.bfloat16),
            pltpu.VMEM((2, 256, 256), jnp.bfloat16),
            pltpu.VMEM((2 * TR * NP, 128), jnp.float32),
            dma((NQ,)), dma((NQ,)),
            dma((NQ, 24)), dma((NQ, 24)),
            dma((NQ, 10)), dma((NQ, 10)),
            dma((NQ, 6)), dma((NQ, 6)),
            dma((NQ, 2 * NY)), dma((NQ, 2 * NY)),
            dma((2, 12)), dma((2, 12)),
            dma((2,)),
            dma,
        ],
        compiler_params=pltpu.CompilerParams(
            collective_id=0, has_side_effects=True, vmem_limit_bytes=53 * 2**20
        ),
        name="tiles_and_coherence",
    )(dest, shift, epochs, x)


def local(radar_echoes, destination_panel, panel_line_shift, epoch_couples):
    dest, shift = destination_panel.reshape(1, BLK), panel_line_shift.reshape(1, BLK)
    return main_call(dest, shift, epoch_couples.T, radar_echoes)


def solution(mesh):
    in_specs = (P("tile", None, "date", None, None), P("tile", None), P("tile"), P())
    out_specs = P("tile", "date", None)
    return jax.shard_map(local, mesh=mesh, in_specs=in_specs, out_specs=out_specs, check_vma=False)
```

```python
import functools

import jax
import jax.numpy as jnp
from jax import lax
from jax.experimental import pallas as pl
from jax.experimental.pallas import tpu as pltpu
from jax.sharding import PartitionSpec as P

NX, NZ, NY = 4, 8, 4
NT = NX * NZ
TR = 256
BR = 16
CAP = 3
BLK = 64
NQ = 8
KS = CAP * BR * 2
KP = 128
NP = 8
MSG = 2 * TR + 16
PIECE = TR + 16
SLOT = (5, 4, 2, 1, 6, 7, 0, 3)
LEVELS = 32000.0
MESH = pl.DeviceIdType.MESH


def power_of(top):
    return jnp.clip(jnp.ceil(jnp.log2(jnp.maximum(top, 1e-30))), -100.0, 100.0)


def encode(v, scale):
    y = jnp.abs(v) * scale
    y = y * lax.rsqrt(jnp.maximum(y, 1e-30))
    y = y * lax.rsqrt(jnp.maximum(y, 1e-15))
    m = (y * LEVELS + 0.5).astype(jnp.int32)
    return jnp.where(v < 0, -m, m).astype(jnp.int16)


def decode(code, scale):
    f = code.astype(jnp.int32).astype(jnp.float32) * (1.0 / LEVELS)
    f = f * jnp.abs(f)
    f = f * jnp.abs(f)
    return f * scale


def scale_of(power):
    return jnp.exp2(power.astype(jnp.int32).astype(jnp.float32)[0:1, :])


def main_kernel(
    dest_ref, shift_ref, ep_ref, x_ref, out_ref,
    table, listed, koff_ref, held, zb, got, kof, place, sent, came, total, fall0, fall1, prod, split, acc, bands, result,
    in_sem, own_sem, xs_sem, xr_sem, zs_sem, zr_sem, ys_sem, yr_sem, cs_sem, cr_sem, ks_sem, kr_sem, out_sem, table_sem,
):
    d = lax.axis_index("date")
    t = lax.axis_index("tile")
    y, core = d // 2, lax.rem(d, 2)
    x, z = t // NZ, lax.rem(t, NZ)
    partner = (y * 2 + 1 - core, t)

    def at(dx, dz):
        return (d, lax.rem(x + dx, NX) * NZ + lax.rem(z + dz + NZ, NZ))

    def at_y(k):
        return (lax.rem(y + k, NY) * 2 + core, t)

    def load(q):
        half, date = divmod(q, 4)
        return pltpu.make_async_copy(
            x_ref.at[:, :, date, :, pl.ds(half * 128, 128)], held.at[pl.ds(q * BLK, BLK)], in_sem.at[q]
        )

    for q in range(NQ):
        load(q).start()

    @pl.loop(0, NQ)
    def _(q):
        for j in range(NZ):
            for s in range(NX):
                got[q, j, s * KP + KS : (s + 1) * KP, :] = jnp.zeros((KP - KS, 128), jnp.bfloat16)

    barrier = pltpu.get_barrier_semaphore()
    peers = [at(1, 0), at(2, 0), at(3, 0), at_y(1), at_y(2), at_y(3), partner]
    peers += [at(k, way) for k in range(NX) for way in (1, -1)]
    for peer in peers:
        pl.semaphore_signal(barrier, 1, device_id=peer, device_id_type=MESH)
    r = lax.broadcasted_iota(jnp.int32, (BLK, BLK), 0)
    c = lax.broadcasted_iota(jnp.int32, (BLK, BLK), 1)
    dest = dest_ref[...]
    along = jnp.broadcast_to(dest, (BLK, BLK)).astype(jnp.float32)
    shifts = jnp.broadcast_to(shift_ref[...], (BLK, BLK)).astype(jnp.float32)
    down = jnp.sum(jnp.where(r == c, along, 0.0), axis=1, keepdims=True)
    shift = jnp.sum(jnp.where(r == c, shifts, 0.0), axis=1, keepdims=True)
    rank = jnp.sum(jnp.where((down == along) & (c < r), 1.0, 0.0), axis=1, keepdims=True)
    lane = lax.broadcasted_iota(jnp.int32, (BLK, 128), 1)
    number = lax.broadcasted_iota(jnp.int32, (BLK, 128), 0)
    chosen = (lane >> 5).astype(jnp.float32) == rank
    off = (dest & (NZ - 1)) - z
    hit = jnp.zeros((BLK, BLK), jnp.float32)
    for par in range(2):
        turn = (off if par == 0 else -off) & (NZ - 1)
        index = par * NT + (dest - (dest & (NZ - 1)))
        for n, slot in enumerate(SLOT):
            index = index + jnp.where(turn == n, slot, 0)
        hit = hit + jnp.where(r == index, 1.0, 0.0)
    hit = hit.astype(jnp.bfloat16)
    first = jnp.where(chosen, (number + 1).astype(jnp.float32), 0.0).astype(jnp.bfloat16)
    second = jnp.where(chosen, shift + 1.0, 0.0).astype(jnp.bfloat16)
    listed[...] = jnp.dot(hit, first, preferred_element_type=jnp.float32).astype(jnp.int32) - 1
    start = jnp.dot(hit, second, preferred_element_type=jnp.float32).astype(jnp.int32)
    goals = jnp.where(start > 0, start - 1 + ((lane & 31) >> 1) + TR * (lane & 1), -1)
    for n in range(2 * NT):
        koff_ref[n] = goals[n : n + 1, :]
    table_copy = pltpu.make_async_copy(listed, table, table_sem)
    table_copy.start()

    pl.semaphore_wait(barrier, len(peers))

    def remote(src, dst, ssem, rsem, dev):
        return pltpu.make_async_remote_copy(
            src_ref=src, dst_ref=dst, send_sem=ssem, recv_sem=rsem, device_id=dev, device_id_type=MESH
        )

    def way_of(q):
        return 1 - 2 * lax.rem(q, 2)

    def koff_copies(par):
        copies = []
        for k in (1, 3, 2):
            there = lax.rem(x + k, NX)
            copies.append(remote(
                koff_ref.at[pl.ds(par * NT + there * NZ, 6)], kof.at[par, x, pl.ds(0, 6)],
                ks_sem.at[par, k], kr_sem.at[par, k], at(k, 0),
            ))
        for m, way in ((6, 1 - 2 * par), (7, 2 * par - 1)):
            for k in range(NX):
                there, n = lax.rem(x + k, NX), 4 * (m - 5) + k
                copies.append(remote(
                    koff_ref.at[par * NT + there * NZ + m], kof.at[par, x, m],
                    ks_sem.at[par, n], kr_sem.at[par, n], at(k, way),
                ))
        return copies

    def x_group(q, g):
        rows = pl.ds(pl.multiple_of(x * KP, KP), KS)
        copies = []
        if g > 0:
            for k in (1, 3, 2):
                first, n = lax.rem(x + k, NX) * NZ + 2 * g - 2, 8 + 4 * g + k
                copies.append(remote(
                    zb.at[q, pl.ds(first, 2)], got.at[q, pl.ds(2 * g - 2, 2), rows],
                    xs_sem.at[q, n], xr_sem.at[q, n], at(k, 0),
                ))
            return copies
        for m, way in ((6, way_of(q)), (7, -way_of(q))):
            for k in range(NX):
                there, n = lax.rem(x + k, NX), 4 * (m - 5) + k
                copies.append(remote(
                    zb.at[q, there * NZ + m], got.at[q, m, rows],
                    xs_sem.at[q, n], xr_sem.at[q, n], at(k, way),
                ))
        return copies

    def own_copy(q):
        return pltpu.make_async_copy(
            zb.at[q, pl.ds(x * NZ, 6)], got.at[q, pl.ds(0, 6), pl.ds(pl.multiple_of(x * KP, KP), KS)],
            own_sem.at[q],
        )

    for par in range(2):
        for copy in koff_copies(par):
            copy.start()
    for q in range(NQ):
        load(q).wait()
    table_copy.wait()

    blocks = held.reshape(NQ * BLK, 2 * BR, 128)

    def send_blocks(q):
        par = lax.rem(q, 2)

        @pl.loop(0, NT)
        def _(i):
            for k in range(CAP):
                b = table[par * NT + i, k * 32]
                v = blocks[q * BLK + jnp.minimum(jnp.maximum(b, 0), BLK - 1)]
                zb[q, i, k * 32 : (k + 1) * 32, :] = jnp.where(b >= 0, v, jnp.zeros_like(v))

        for g in range(4):
            for copy in x_group(q, g):
                copy.start()
        own_copy(q).start()

    def build(par):
        kof[par, x, 0:6] = koff_ref[pl.ds(par * NT + x * NZ, 6)]
        for copy in koff_copies(par):
            copy.wait()

        @pl.loop(0, NZ)
        def _(j):
            for s in range(NX):
                goal = kof[par, s, j]
                for i in range(4):
                    row = lax.broadcasted_iota(jnp.int32, (128, 128), 0) + i * 128
                    hit = jnp.where(row == goal, 1.0, 0.0).astype(jnp.bfloat16)
                    place[par, j, i * 128 : (i + 1) * 128, s * 128 : (s + 1) * 128] = hit

    @pl.loop(0, 3)
    def _(q):
        send_blocks(q)

    build(0)
    build(1)
    for half in range(2):
        i = lax.broadcasted_iota(jnp.int32, (256, 256), 0)
        j = lax.broadcasted_iota(jnp.int32, (256, 256), 1)
        near = jnp.abs((i & 127) + half * 128 - j) <= 7
        bands[half] = jnp.where(near, 1.0, 0.0).astype(jnp.bfloat16)
    prod[...] = jnp.zeros_like(prod)

    def part(q, j, i):
        return jnp.dot(
            place[lax.rem(q, 2), j, i * 128 : (i + 1) * 128, :], got[q, j],
            preferred_element_type=jnp.float32,
        )

    def z_copy(q, n, h, way):
        piece = pl.ds(h * PIECE, PIECE if h == 0 else TR)
        return remote(
            sent.at[q, n, piece], came.at[q, n, piece], zs_sem.at[q, 2 * n + h], zr_sem.at[q, 2 * n + h], at(0, way)
        )

    def own_part(q, slots, at_total):
        top = jnp.zeros((8, 128), jnp.float32)
        for i in range(4):
            v = part(q, slots[0], i)
            for slot in slots[1:]:
                v = v + part(q, slot, i)
            total[at_total, i * 128 : (i + 1) * 128, :] = v
            top = jnp.maximum(top, jnp.max(jnp.abs(v).reshape(16, 8, 128), axis=0))
        return jnp.max(top, axis=0, keepdims=True)

    def hop(q, units):
        tops = [own_part(q, slots, u) for u, (_, slots, _, _) in enumerate(units)]
        scales = [None] * len(units)
        for h in range(2):
            for u, (way, _, taken, n) in enumerate(units):
                if taken is not None:
                    z_copy(q, taken, h, way).wait_recv()
                if h == 0:
                    arrived = None
                    if taken is not None:
                        arrived = scale_of(came[q, taken, 2 * 128 : PIECE, :])
                        tops[u] = tops[u] + arrived
                    power = power_of(tops[u])
                    sent[q, n, 2 * 128 : PIECE, :] = (
                        jnp.broadcast_to(power, (16, 128)).astype(jnp.int32).astype(jnp.int16)
                    )
                    scales[u] = (arrived, jnp.exp2(-power))
                arrived, scale = scales[u]
                for part_no in range(2):
                    i = part_no * 2 + h
                    rows = slice(h * PIECE + part_no * 128, h * PIECE + part_no * 128 + 128)
                    v = total[u, i * 128 : (i + 1) * 128, :]
                    if taken is not None:
                        v = v + decode(came[q, taken, rows, :], arrived)
                    sent[q, n, rows, :] = encode(v, scale)
                z_copy(q, n, h, way).start()

    def y_copy(fall, q, k, h):
        mine = fall.at[d * 4 + lax.rem(q, 4), :, pl.ds(h * 128, 128)]
        n = 2 * k - 2 + h
        return remote(mine, mine, ys_sem.at[q, n], yr_sem.at[q, n], at_y(k))

    def core_copy(fall, q, k, h):
        from_d = lax.rem(y - k + NY, NY) * 2 + core
        field = fall.at[from_d * 4 + lax.rem(q, 4), :, pl.ds(h * 128, 128)]
        return remote(field, field, cs_sem.at[q, 2 * k + h], cr_sem.at[q, 2 * k + h], partner)

    def finish(q, fall):
        way = way_of(q)
        own_part(q, (5,), 0)
        scales = [None, None]
        for h in range(2):
            for u, (n, w) in enumerate(((2, way), (4, -way))):
                z_copy(q, n, h, w).wait_recv()
                if h == 0:
                    scales[u] = scale_of(came[q, n, 2 * 128 : PIECE, :])
            for part_no in range(2):
                i = part_no * 2 + h
                rows = slice(h * PIECE + part_no * 128, h * PIECE + part_no * 128 + 128)
                v = total[0, i * 128 : (i + 1) * 128, :]
                v = v + (decode(came[q, 2, rows, :], scales[0]) + decode(came[q, 4, rows, :], scales[1]))
                fall[d * 4 + lax.rem(q, 4), part_no, h * 128 : (h + 1) * 128, :] = v.astype(jnp.bfloat16)
            for k in (1, 3, 2):
                y_copy(fall, q, k, h).start()
            core_copy(fall, q, 0, h).start()

    def forward(q, fall):
        for h in range(2):
            for k in (1, 3, 2):
                y_copy(fall, q, k, h).wait_recv()
                core_copy(fall, q, k, h).start()

    def arrive(q, fall):
        for h in range(2):
            for k in range(NY):
                core_copy(fall, q, k, h).wait_recv()

    def out_copy(side):
        return pltpu.make_async_copy(
            result.reshape(2, TR, NP, 128).at[side],
            out_ref.at[:, :, pl.ds(side * 128, 128)],
            out_sem.at[side],
        )

    def boxes(half, fall, first, number):
        @pl.loop(first, first + number)
        def _(p):
            a = ep_ref[0, d * NP + p]
            e = ep_ref[1, d * NP + p]
            for i in range(4):
                lo = i * 64
                u0 = fall[a, 0, lo : lo + 64, :].astype(jnp.float32)
                u1 = fall[a, 1, lo : lo + 64, :].astype(jnp.float32)
                v0 = fall[e, 0, lo : lo + 64, :].astype(jnp.float32)
                v1 = fall[e, 1, lo : lo + 64, :].astype(jnp.float32)
                prod[0, 8 + lo : 72 + lo, :] = u0 * v0 + u1 * v1
                prod[1, 8 + lo : 72 + lo, :] = u1 * v0 - u0 * v1
                prod[2, 8 + lo : 72 + lo, :] = u0 * u0 + u1 * u1
                prod[3, 8 + lo : 72 + lo, :] = v0 * v0 + v1 * v1
            for f in range(4):
                for i in range(4):
                    lo = i * 64
                    s = prod[f, 5 + lo : 69 + lo, :]
                    for k in range(1, 7):
                        s = s + prod[f, 5 + lo + k : 69 + lo + k, :]
                    high = s.astype(jnp.bfloat16)
                    low = (s - high.astype(jnp.float32)).astype(jnp.bfloat16)
                    split[f, lo : lo + 64, 0:128] = high
                    split[f, lo : lo + 64, 128:256] = low
            for f in range(4):
                r = jnp.dot(split[f], bands[half], preferred_element_type=jnp.float32)
                acc[p, f] = r if half == 0 else acc[p, f] + r
            if half == 1:
                for i in range(8):
                    lo = i * 32
                    re, im, pa, pe = [acc[p, f, lo : lo + 32, :] for f in range(4)]
                    n = re * re + im * im
                    c = n * lax.rsqrt(jnp.maximum(n, 1e-30)) * lax.rsqrt(jnp.maximum(pa * pe, 1.0))
                    for side in range(2):
                        rows = pl.ds(side * NP * TR + lo * NP + p, 32, stride=NP)
                        result[rows, :] = c[:, side * 128 : (side + 1) * 128]

    @pl.loop(0, NQ + 3)
    def _(step):
        @pl.when(step < NQ)
        def _():
            for copy in x_group(step, 0) + x_group(step, 1):
                copy.wait_recv()
            own_copy(step).wait()
            hop(step, ((way_of(step), (1, 6), None, 0), (-way_of(step), (0, 7), None, 3)))

        @pl.when((step >= 1) & (step < NQ + 1))
        def _():
            for copy in x_group(step - 1, 3):
                copy.wait_recv()
            hop(step - 1, ((way_of(step - 1), (4,), 1, 2),))

        @pl.when(step + 3 < NQ)
        def _():
            send_blocks(step + 3)

        for half, fall in enumerate((fall0, fall1)):
            first = half * 4

            @pl.when((step >= first + 2) & (step < first + 6))
            def _(fall=fall):
                forward(step - 2, fall)

            @pl.when((step >= first + 3) & (step < first + 7))
            def _(fall=fall):
                arrive(step - 3, fall)

        @pl.when(step < NQ)
        def _():
            for copy in x_group(step, 2):
                copy.wait_recv()
            hop(step, ((way_of(step), (2,), 0, 1), (-way_of(step), (3,), 3, 4)))

        for half, fall in enumerate((fall0, fall1)):
            first = half * 4

            @pl.when((step >= first + 1) & (step < first + 5))
            def _(fall=fall):
                finish(step - 1, fall)

        @pl.when((step == 6) | (step == 8))
        def _():
            boxes(0, fall0, (step - 6) * 2, 4)

    boxes(1, fall1, 0, NP)
    for side in range(2):
        out_copy(side).start()

    @pl.loop(0, NQ)
    def _(q):
        for g in range(4):
            for copy in x_group(q, g):
                copy.wait_send()
        for h in range(2):
            for n in range(5):
                z_copy(q, n, h, 1).wait_send()
            for k in (1, 2, 3):
                y_copy(fall0, q, k, h).wait_send()
            for k in range(NY):
                core_copy(fall0, q, k, h).wait_send()

    for side in range(2):
        out_copy(side).wait()


def main_call(dest, shift, epochs, x):
    dma = pltpu.SemaphoreType.DMA
    field = pltpu.VMEM((32, 2, TR, 128), jnp.bfloat16)
    vmem = pl.BlockSpec(memory_space=pltpu.VMEM)
    return pl.pallas_call(
        main_kernel,
        out_shape=jax.ShapeDtypeStruct((TR, NP, 256), jnp.float32),
        in_specs=[vmem, vmem, pl.BlockSpec(memory_space=pltpu.SMEM), pl.BlockSpec(memory_space=pl.ANY)],
        out_specs=pl.BlockSpec(memory_space=pl.ANY),
        scratch_shapes=[
            pltpu.SMEM((2 * NT, 128), jnp.int32),
            pltpu.VMEM((2 * NT, 128), jnp.int32),
            pltpu.VMEM((2 * NT, 1, 128), jnp.int32),
            pltpu.VMEM((NQ * BLK, BR, 2, 128), jnp.bfloat16),
            pltpu.VMEM((NQ, NT, KS, 128), jnp.bfloat16),
            pltpu.VMEM((NQ, NZ, NX * KP, 128), jnp.bfloat16),
            pltpu.VMEM((2, NX, NZ, 1, 128), jnp.int32),
            pltpu.VMEM((2, NZ, 2 * TR, NX * KP), jnp.bfloat16),
            pltpu.VMEM((NQ, 5, MSG, 128), jnp.int16),
            pltpu.VMEM((NQ, 5, MSG, 128), jnp.int16),
            pltpu.VMEM((2, 2 * TR, 128), jnp.float32),
            field,
            field,
            pltpu.VMEM((4, TR + 16, 128), jnp.float32),
            pltpu.VMEM((4, TR, 256), jnp.bfloat16),
            pltpu.VMEM((NP, 4, TR, 256), jnp.float32),
            pltpu.VMEM((2, 256, 256), jnp.bfloat16),
            pltpu.VMEM((2 * TR * NP, 128), jnp.float32),
            dma((NQ,)), dma((NQ,)),
            dma((NQ, 24)), dma((NQ, 24)),
            dma((NQ, 10)), dma((NQ, 10)),
            dma((NQ, 6)), dma((NQ, 6)),
            dma((NQ, 2 * NY)), dma((NQ, 2 * NY)),
            dma((2, 12)), dma((2, 12)),
            dma((2,)),
            dma,
        ],
        compiler_params=pltpu.CompilerParams(
            collective_id=0, has_side_effects=True, vmem_limit_bytes=58 * 2**20
        ),
        name="tiles_and_coherence",
    )(dest, shift, epochs, x)


def local(radar_echoes, destination_panel, panel_line_shift, epoch_couples):
    dest, shift = destination_panel.reshape(1, BLK), panel_line_shift.reshape(1, BLK)
    return main_call(dest, shift, epoch_couples.T, radar_echoes)


def solution(mesh):
    in_specs = (P("tile", None, "date", None, None), P("tile", None), P("tile"), P())
    out_specs = P("tile", "date", None)
    return jax.shard_map(local, mesh=mesh, in_specs=in_specs, out_specs=out_specs, check_vma=False)
```

```python
import functools

import jax
import jax.numpy as jnp
from jax import lax
from jax.experimental import pallas as pl
from jax.experimental.pallas import tpu as pltpu
from jax.sharding import PartitionSpec as P

NX, NZ, NY = 4, 8, 4
NT = NX * NZ
TR = 256
BR = 16
CAP = 3
BLK = 64
NQ = 8
KS = CAP * BR * 2
KP = 128
NP = 8
MSG = 2 * TR + 16
PIECE = TR + 16
SLOT = (5, 4, 2, 1, 6, 7, 0, 3)
LEVELS = 32000.0
MESH = pl.DeviceIdType.MESH


def power_of(top):
    return jnp.clip(jnp.ceil(jnp.log2(jnp.maximum(top, 1e-30))), -100.0, 100.0)


def encode(v, scale):
    y = jnp.abs(v) * scale
    y = y * lax.rsqrt(jnp.maximum(y, 1e-30))
    y = y * lax.rsqrt(jnp.maximum(y, 1e-15))
    m = (y * LEVELS + 0.5).astype(jnp.int32)
    return jnp.where(v < 0, -m, m).astype(jnp.int16)


def decode(code, scale):
    f = code.astype(jnp.int32).astype(jnp.float32) * (1.0 / LEVELS)
    f = f * jnp.abs(f)
    f = f * jnp.abs(f)
    return f * scale


def scale_of(power):
    return jnp.exp2(power.astype(jnp.int32).astype(jnp.float32)[0:1, :])


def main_kernel(
    dest_ref, shift_ref, ep_ref, x_ref, out_ref,
    table, listed, koff_ref, held, zb, got, kof, place, sent, came, total, fall0, fall1, prod, split, acc, bands, result,
    in_sem, own_sem, xs_sem, xr_sem, zs_sem, zr_sem, ys_sem, yr_sem, cs_sem, cr_sem, ks_sem, kr_sem, out_sem, table_sem,
):
    d = lax.axis_index("date")
    t = lax.axis_index("tile")
    y, core = d // 2, lax.rem(d, 2)
    x, z = t // NZ, lax.rem(t, NZ)
    partner = (y * 2 + 1 - core, t)

    def at(dx, dz):
        return (d, lax.rem(x + dx, NX) * NZ + lax.rem(z + dz + NZ, NZ))

    def at_y(k):
        return (lax.rem(y + k, NY) * 2 + core, t)

    def load(q):
        half, date = divmod(q, 4)
        return pltpu.make_async_copy(
            x_ref.at[:, :, date, :, pl.ds(half * 128, 128)], held.at[pl.ds(q * BLK, BLK)], in_sem.at[q]
        )

    for q in range(NQ):
        load(q).start()

    @pl.loop(0, NQ)
    def _(q):
        for j in range(NZ):
            for s in range(NX):
                got[q, j, s * KP + KS : (s + 1) * KP, :] = jnp.zeros((KP - KS, 128), jnp.bfloat16)

    barrier = pltpu.get_barrier_semaphore()
    peers = [at(1, 0), at(2, 0), at(3, 0), at_y(1), at_y(2), at_y(3), partner]
    peers += [at(k, way) for k in range(NX) for way in (1, -1)]
    for peer in peers:
        pl.semaphore_signal(barrier, 1, device_id=peer, device_id_type=MESH)
    r = lax.broadcasted_iota(jnp.int32, (BLK, BLK), 0)
    c = lax.broadcasted_iota(jnp.int32, (BLK, BLK), 1)
    dest = dest_ref[...]
    along = jnp.broadcast_to(dest, (BLK, BLK)).astype(jnp.float32)
    shifts = jnp.broadcast_to(shift_ref[...], (BLK, BLK)).astype(jnp.float32)
    down = jnp.sum(jnp.where(r == c, along, 0.0), axis=1, keepdims=True)
    shift = jnp.sum(jnp.where(r == c, shifts, 0.0), axis=1, keepdims=True)
    rank = jnp.sum(jnp.where((down == along) & (c < r), 1.0, 0.0), axis=1, keepdims=True)
    lane = lax.broadcasted_iota(jnp.int32, (BLK, 128), 1)
    number = lax.broadcasted_iota(jnp.int32, (BLK, 128), 0)
    chosen = (lane >> 5).astype(jnp.float32) == rank
    off = (dest & (NZ - 1)) - z
    hit = jnp.zeros((BLK, BLK), jnp.float32)
    for par in range(2):
        turn = (off if par == 0 else -off) & (NZ - 1)
        index = par * NT + (dest - (dest & (NZ - 1)))
        for n, slot in enumerate(SLOT):
            index = index + jnp.where(turn == n, slot, 0)
        hit = hit + jnp.where(r == index, 1.0, 0.0)
    hit = hit.astype(jnp.bfloat16)
    first = jnp.where(chosen, (number + 1).astype(jnp.float32), 0.0).astype(jnp.bfloat16)
    second = jnp.where(chosen, shift + 1.0, 0.0).astype(jnp.bfloat16)
    listed[...] = jnp.dot(hit, first, preferred_element_type=jnp.float32).astype(jnp.int32) - 1
    start = jnp.dot(hit, second, preferred_element_type=jnp.float32).astype(jnp.int32)
    goals = jnp.where(start > 0, start - 1 + ((lane & 31) >> 1) + TR * (lane & 1), -1)
    for n in range(2 * NT):
        koff_ref[n] = goals[n : n + 1, :]
    table_copy = pltpu.make_async_copy(listed, table, table_sem)
    table_copy.start()

    pl.semaphore_wait(barrier, len(peers))

    def remote(src, dst, ssem, rsem, dev):
        return pltpu.make_async_remote_copy(
            src_ref=src, dst_ref=dst, send_sem=ssem, recv_sem=rsem, device_id=dev, device_id_type=MESH
        )

    def way_of(q):
        return 1 - 2 * lax.rem(q, 2)

    def koff_copies(par):
        copies = []
        for k in (2, 1, 3):
            there = lax.rem(x + k, NX)
            copies.append(remote(
                koff_ref.at[pl.ds(par * NT + there * NZ, 6)], kof.at[par, x, pl.ds(0, 6)],
                ks_sem.at[par, k], kr_sem.at[par, k], at(k, 0),
            ))
        for m, way in ((6, 1 - 2 * par), (7, 2 * par - 1)):
            for k in range(NX):
                there, n = lax.rem(x + k, NX), 4 * (m - 5) + k
                copies.append(remote(
                    koff_ref.at[par * NT + there * NZ + m], kof.at[par, x, m],
                    ks_sem.at[par, n], kr_sem.at[par, n], at(k, way),
                ))
        return copies

    def x_group(q, g):
        rows = pl.ds(pl.multiple_of(x * KP, KP), KS)
        copies = []
        if g > 0:
            for k in (2, 1, 3):
                first, n = lax.rem(x + k, NX) * NZ + 2 * g - 2, 8 + 4 * g + k
                copies.append(remote(
                    zb.at[q, pl.ds(first, 2)], got.at[q, pl.ds(2 * g - 2, 2), rows],
                    xs_sem.at[q, n], xr_sem.at[q, n], at(k, 0),
                ))
            return copies
        for m, way in ((6, way_of(q)), (7, -way_of(q))):
            for k in range(NX):
                there, n = lax.rem(x + k, NX), 4 * (m - 5) + k
                copies.append(remote(
                    zb.at[q, there * NZ + m], got.at[q, m, rows],
                    xs_sem.at[q, n], xr_sem.at[q, n], at(k, way),
                ))
        return copies

    def own_copy(q):
        return pltpu.make_async_copy(
            zb.at[q, pl.ds(x * NZ, 6)], got.at[q, pl.ds(0, 6), pl.ds(pl.multiple_of(x * KP, KP), KS)],
            own_sem.at[q],
        )

    for par in range(2):
        for copy in koff_copies(par):
            copy.start()
    for q in range(NQ):
        load(q).wait()
    table_copy.wait()

    blocks = held.reshape(NQ * BLK, 2 * BR, 128)

    def send_blocks(q):
        par = lax.rem(q, 2)

        @pl.loop(0, NT)
        def _(i):
            for k in range(CAP):
                b = table[par * NT + i, k * 32]
                v = blocks[q * BLK + jnp.minimum(jnp.maximum(b, 0), BLK - 1)]
                zb[q, i, k * 32 : (k + 1) * 32, :] = jnp.where(b >= 0, v, jnp.zeros_like(v))

        for g in range(4):
            for copy in x_group(q, g):
                copy.start()
        own_copy(q).start()

    def build(par):
        kof[par, x, 0:6] = koff_ref[pl.ds(par * NT + x * NZ, 6)]
        for copy in koff_copies(par):
            copy.wait()

        @pl.loop(0, NZ)
        def _(j):
            for s in range(NX):
                goal = kof[par, s, j]
                for i in range(4):
                    row = lax.broadcasted_iota(jnp.int32, (128, 128), 0) + i * 128
                    hit = jnp.where(row == goal, 1.0, 0.0).astype(jnp.bfloat16)
                    place[par, j, i * 128 : (i + 1) * 128, s * 128 : (s + 1) * 128] = hit

    @pl.loop(0, 3)
    def _(q):
        send_blocks(q)

    build(0)
    build(1)
    for half in range(2):
        i = lax.broadcasted_iota(jnp.int32, (256, 256), 0)
        j = lax.broadcasted_iota(jnp.int32, (256, 256), 1)
        near = jnp.abs((i & 127) + half * 128 - j) <= 7
        bands[half] = jnp.where(near, 1.0, 0.0).astype(jnp.bfloat16)
    prod[...] = jnp.zeros_like(prod)

    def part(q, j, i):
        return jnp.dot(
            place[lax.rem(q, 2), j, i * 128 : (i + 1) * 128, :], got[q, j],
            preferred_element_type=jnp.float32,
        )

    def z_copy(q, n, h, way):
        piece = pl.ds(h * PIECE, PIECE if h == 0 else TR)
        return remote(
            sent.at[q, n, piece], came.at[q, n, piece], zs_sem.at[q, 2 * n + h], zr_sem.at[q, 2 * n + h], at(0, way)
        )

    def own_part(q, slots, at_total):
        top = jnp.zeros((8, 128), jnp.float32)
        for i in range(4):
            v = part(q, slots[0], i)
            for slot in slots[1:]:
                v = v + part(q, slot, i)
            total[at_total, i * 128 : (i + 1) * 128, :] = v
            top = jnp.maximum(top, jnp.max(jnp.abs(v).reshape(16, 8, 128), axis=0))
        return jnp.max(top, axis=0, keepdims=True)

    def hop(q, units):
        tops = [own_part(q, slots, u) for u, (_, slots, _, _) in enumerate(units)]
        scales = [None] * len(units)
        for h in range(2):
            for u, (way, _, taken, n) in enumerate(units):
                if taken is not None:
                    z_copy(q, taken, h, way).wait_recv()
                if h == 0:
                    arrived = None
                    if taken is not None:
                        arrived = scale_of(came[q, taken, 2 * 128 : PIECE, :])
                        tops[u] = tops[u] + arrived
                    power = power_of(tops[u])
                    sent[q, n, 2 * 128 : PIECE, :] = (
                        jnp.broadcast_to(power, (16, 128)).astype(jnp.int32).astype(jnp.int16)
                    )
                    scales[u] = (arrived, jnp.exp2(-power))
                arrived, scale = scales[u]
                for part_no in range(2):
                    i = part_no * 2 + h
                    rows = slice(h * PIECE + part_no * 128, h * PIECE + part_no * 128 + 128)
                    v = total[u, i * 128 : (i + 1) * 128, :]
                    if taken is not None:
                        v = v + decode(came[q, taken, rows, :], arrived)
                    sent[q, n, rows, :] = encode(v, scale)
                z_copy(q, n, h, way).start()

    def y_copy(fall, q, k, h):
        mine = fall.at[d * 4 + lax.rem(q, 4), :, pl.ds(h * 128, 128)]
        n = 2 * k - 2 + h
        return remote(mine, mine, ys_sem.at[q, n], yr_sem.at[q, n], at_y(k))

    def core_copy(fall, q, k, h):
        from_d = lax.rem(y - k + NY, NY) * 2 + core
        field = fall.at[from_d * 4 + lax.rem(q, 4), :, pl.ds(h * 128, 128)]
        return remote(field, field, cs_sem.at[q, 2 * k + h], cr_sem.at[q, 2 * k + h], partner)

    def finish(q, fall):
        way = way_of(q)
        own_part(q, (5,), 0)
        scales = [None, None]
        for h in range(2):
            for u, (n, w) in enumerate(((2, way), (4, -way))):
                z_copy(q, n, h, w).wait_recv()
                if h == 0:
                    scales[u] = scale_of(came[q, n, 2 * 128 : PIECE, :])
            for part_no in range(2):
                i = part_no * 2 + h
                rows = slice(h * PIECE + part_no * 128, h * PIECE + part_no * 128 + 128)
                v = total[0, i * 128 : (i + 1) * 128, :]
                v = v + (decode(came[q, 2, rows, :], scales[0]) + decode(came[q, 4, rows, :], scales[1]))
                fall[d * 4 + lax.rem(q, 4), part_no, h * 128 : (h + 1) * 128, :] = v.astype(jnp.bfloat16)
            for k in (2, 1, 3):
                y_copy(fall, q, k, h).start()
            core_copy(fall, q, 0, h).start()

    def forward(q, fall):
        for h in range(2):
            for k in (2, 1, 3):
                y_copy(fall, q, k, h).wait_recv()
                core_copy(fall, q, k, h).start()

    def arrive(q, fall):
        for h in range(2):
            for k in range(NY):
                core_copy(fall, q, k, h).wait_recv()

    def out_copy(side):
        return pltpu.make_async_copy(
            result.reshape(2, TR, NP, 128).at[side],
            out_ref.at[:, :, pl.ds(side * 128, 128)],
            out_sem.at[side],
        )

    def boxes(half, fall, first, number):
        @pl.loop(first, first + number)
        def _(p):
            a = ep_ref[0, d * NP + p]
            e = ep_ref[1, d * NP + p]
            for i in range(4):
                lo = i * 64
                u0 = fall[a, 0, lo : lo + 64, :].astype(jnp.float32)
                u1 = fall[a, 1, lo : lo + 64, :].astype(jnp.float32)
                v0 = fall[e, 0, lo : lo + 64, :].astype(jnp.float32)
                v1 = fall[e, 1, lo : lo + 64, :].astype(jnp.float32)
                prod[0, 8 + lo : 72 + lo, :] = u0 * v0 + u1 * v1
                prod[1, 8 + lo : 72 + lo, :] = u1 * v0 - u0 * v1
                prod[2, 8 + lo : 72 + lo, :] = u0 * u0 + u1 * u1
                prod[3, 8 + lo : 72 + lo, :] = v0 * v0 + v1 * v1
            for f in range(4):
                for i in range(4):
                    lo = i * 64
                    s = prod[f, 5 + lo : 69 + lo, :]
                    for k in range(1, 7):
                        s = s + prod[f, 5 + lo + k : 69 + lo + k, :]
                    high = s.astype(jnp.bfloat16)
                    low = (s - high.astype(jnp.float32)).astype(jnp.bfloat16)
                    split[f, lo : lo + 64, 0:128] = high
                    split[f, lo : lo + 64, 128:256] = low
            for f in range(4):
                r = jnp.dot(split[f], bands[half], preferred_element_type=jnp.float32)
                acc[p, f] = r if half == 0 else acc[p, f] + r
            if half == 1:
                for i in range(8):
                    lo = i * 32
                    re, im, pa, pe = [acc[p, f, lo : lo + 32, :] for f in range(4)]
                    n = re * re + im * im
                    c = n * lax.rsqrt(jnp.maximum(n, 1e-30)) * lax.rsqrt(jnp.maximum(pa * pe, 1.0))
                    for side in range(2):
                        rows = pl.ds(side * NP * TR + lo * NP + p, 32, stride=NP)
                        result[rows, :] = c[:, side * 128 : (side + 1) * 128]

    @pl.loop(0, NQ + 3)
    def _(step):
        @pl.when(step < NQ)
        def _():
            for copy in x_group(step, 0) + x_group(step, 1):
                copy.wait_recv()
            own_copy(step).wait()
            hop(step, ((way_of(step), (1, 6), None, 0), (-way_of(step), (0, 7), None, 3)))

        @pl.when((step >= 1) & (step < NQ + 1))
        def _():
            for copy in x_group(step - 1, 3):
                copy.wait_recv()
            hop(step - 1, ((way_of(step - 1), (4,), 1, 2),))

        @pl.when(step + 3 < NQ)
        def _():
            send_blocks(step + 3)

        for half, fall in enumerate((fall0, fall1)):
            first = half * 4

            @pl.when((step >= first + 2) & (step < first + 6))
            def _(fall=fall):
                forward(step - 2, fall)

            @pl.when((step >= first + 3) & (step < first + 7))
            def _(fall=fall):
                arrive(step - 3, fall)

        @pl.when(step < NQ)
        def _():
            for copy in x_group(step, 2):
                copy.wait_recv()
            hop(step, ((way_of(step), (2,), 0, 1), (-way_of(step), (3,), 3, 4)))

        for half, fall in enumerate((fall0, fall1)):
            first = half * 4

            @pl.when((step >= first + 1) & (step < first + 5))
            def _(fall=fall):
                finish(step - 1, fall)

        @pl.when((step == 6) | (step == 8))
        def _():
            boxes(0, fall0, (step - 6) * 2, 4)

    boxes(1, fall1, 0, NP)
    for side in range(2):
        out_copy(side).start()

    @pl.loop(0, NQ)
    def _(q):
        for g in range(4):
            for copy in x_group(q, g):
                copy.wait_send()
        for h in range(2):
            for n in range(5):
                z_copy(q, n, h, 1).wait_send()
            for k in (1, 2, 3):
                y_copy(fall0, q, k, h).wait_send()
            for k in range(NY):
                core_copy(fall0, q, k, h).wait_send()

    for side in range(2):
        out_copy(side).wait()


def main_call(dest, shift, epochs, x):
    dma = pltpu.SemaphoreType.DMA
    field = pltpu.VMEM((32, 2, TR, 128), jnp.bfloat16)
    vmem = pl.BlockSpec(memory_space=pltpu.VMEM)
    return pl.pallas_call(
        main_kernel,
        out_shape=jax.ShapeDtypeStruct((TR, NP, 256), jnp.float32),
        in_specs=[vmem, vmem, pl.BlockSpec(memory_space=pltpu.SMEM), pl.BlockSpec(memory_space=pl.ANY)],
        out_specs=pl.BlockSpec(memory_space=pl.ANY),
        scratch_shapes=[
            pltpu.SMEM((2 * NT, 128), jnp.int32),
            pltpu.VMEM((2 * NT, 128), jnp.int32),
            pltpu.VMEM((2 * NT, 1, 128), jnp.int32),
            pltpu.VMEM((NQ * BLK, BR, 2, 128), jnp.bfloat16),
            pltpu.VMEM((NQ, NT, KS, 128), jnp.bfloat16),
            pltpu.VMEM((NQ, NZ, NX * KP, 128), jnp.bfloat16),
            pltpu.VMEM((2, NX, NZ, 1, 128), jnp.int32),
            pltpu.VMEM((2, NZ, 2 * TR, NX * KP), jnp.bfloat16),
            pltpu.VMEM((NQ, 5, MSG, 128), jnp.int16),
            pltpu.VMEM((NQ, 5, MSG, 128), jnp.int16),
            pltpu.VMEM((2, 2 * TR, 128), jnp.float32),
            field,
            field,
            pltpu.VMEM((4, TR + 16, 128), jnp.float32),
            pltpu.VMEM((4, TR, 256), jnp.bfloat16),
            pltpu.VMEM((NP, 4, TR, 256), jnp.float32),
            pltpu.VMEM((2, 256, 256), jnp.bfloat16),
            pltpu.VMEM((2 * TR * NP, 128), jnp.float32),
            dma((NQ,)), dma((NQ,)),
            dma((NQ, 24)), dma((NQ, 24)),
            dma((NQ, 10)), dma((NQ, 10)),
            dma((NQ, 6)), dma((NQ, 6)),
            dma((NQ, 2 * NY)), dma((NQ, 2 * NY)),
            dma((2, 12)), dma((2, 12)),
            dma((2,)),
            dma,
        ],
        compiler_params=pltpu.CompilerParams(
            collective_id=0, has_side_effects=True, vmem_limit_bytes=58 * 2**20
        ),
        name="tiles_and_coherence",
    )(dest, shift, epochs, x)


def local(radar_echoes, destination_panel, panel_line_shift, epoch_couples):
    dest, shift = destination_panel.reshape(1, BLK), panel_line_shift.reshape(1, BLK)
    return main_call(dest, shift, epoch_couples.T, radar_echoes)


def solution(mesh):
    in_specs = (P("tile", None, "date", None, None), P("tile", None), P("tile"), P())
    out_specs = P("tile", "date", None)
    return jax.shard_map(local, mesh=mesh, in_specs=in_specs, out_specs=out_specs, check_vma=False)
```

```python
import functools

import jax
import jax.numpy as jnp
from jax import lax
from jax.experimental import pallas as pl
from jax.experimental.pallas import tpu as pltpu
from jax.sharding import PartitionSpec as P

NX, NZ, NY = 4, 8, 4
NT = NX * NZ
TR = 256
BR = 16
CAP = 3
BLK = 64
NQ = 8
KS = CAP * BR * 2
KP = 128
NP = 8
MSG = 2 * TR + 16
PIECE = TR + 16
SLOT = (5, 4, 2, 1, 6, 7, 0, 3)
LEVELS = 32000.0
MESH = pl.DeviceIdType.MESH


def power_of(top):
    return jnp.clip(jnp.ceil(jnp.log2(jnp.maximum(top, 1e-30))), -100.0, 100.0)


def encode(v, scale):
    y = jnp.abs(v) * scale
    y = y * lax.rsqrt(jnp.maximum(y, 1e-30))
    y = y * lax.rsqrt(jnp.maximum(y, 1e-15))
    m = (y * LEVELS + 0.5).astype(jnp.int32)
    return jnp.where(v < 0, -m, m).astype(jnp.int16)


def decode(code, scale):
    f = code.astype(jnp.int32).astype(jnp.float32) * (1.0 / LEVELS)
    f = f * jnp.abs(f)
    f = f * jnp.abs(f)
    return f * scale


def scale_of(power):
    return jnp.exp2(power.astype(jnp.int32).astype(jnp.float32)[0:1, :])


def main_kernel(
    dest_ref, shift_ref, ep_ref, x_ref, out_ref,
    table, listed, koff_ref, held0, held, zb, got, kof, place, sent, came, total, fall0, fall1, prod, split, acc, bands, result,
    in_sem, own_sem, xs_sem, xr_sem, zs_sem, zr_sem, ys_sem, yr_sem, cs_sem, cr_sem, ks_sem, kr_sem, out_sem, table_sem,
):
    d = lax.axis_index("date")
    t = lax.axis_index("tile")
    y, core = d // 2, lax.rem(d, 2)
    x, z = t // NZ, lax.rem(t, NZ)
    partner = (y * 2 + 1 - core, t)

    def at(dx, dz):
        return (d, lax.rem(x + dx, NX) * NZ + lax.rem(z + dz + NZ, NZ))

    def at_y(k):
        return (lax.rem(y + k, NY) * 2 + core, t)

    def load(q):
        half, date = divmod(q, 4)
        return pltpu.make_async_copy(
            x_ref.at[:, :, date, :, pl.ds(half * 128, 128)],
            held0 if q == 0 else held.at[pl.ds((q - 1) * BLK, BLK)],
            in_sem.at[q],
        )

    for q in range(NQ):
        load(q).start()

    @pl.loop(0, NQ)
    def _(q):
        for j in range(NZ):
            for s in range(NX):
                got[q, j, s * KP + KS : (s + 1) * KP, :] = jnp.zeros((KP - KS, 128), jnp.bfloat16)

    barrier = pltpu.get_barrier_semaphore()
    peers = [at(1, 0), at(2, 0), at(3, 0), at_y(1), at_y(2), at_y(3), partner]
    peers += [at(k, way) for k in range(NX) for way in (1, -1)]
    for peer in peers:
        pl.semaphore_signal(barrier, 1, device_id=peer, device_id_type=MESH)
    r = lax.broadcasted_iota(jnp.int32, (BLK, BLK), 0)
    c = lax.broadcasted_iota(jnp.int32, (BLK, BLK), 1)
    dest = dest_ref[...]
    along = jnp.broadcast_to(dest, (BLK, BLK)).astype(jnp.float32)
    shifts = jnp.broadcast_to(shift_ref[...], (BLK, BLK)).astype(jnp.float32)
    down = jnp.sum(jnp.where(r == c, along, 0.0), axis=1, keepdims=True)
    shift = jnp.sum(jnp.where(r == c, shifts, 0.0), axis=1, keepdims=True)
    rank = jnp.sum(jnp.where((down == along) & (c < r), 1.0, 0.0), axis=1, keepdims=True)
    lane = lax.broadcasted_iota(jnp.int32, (BLK, 128), 1)
    number = lax.broadcasted_iota(jnp.int32, (BLK, 128), 0)
    chosen = (lane >> 5).astype(jnp.float32) == rank
    off = (dest & (NZ - 1)) - z
    hit = jnp.zeros((BLK, BLK), jnp.float32)
    for par in range(2):
        turn = (off if par == 0 else -off) & (NZ - 1)
        index = par * NT + (dest - (dest & (NZ - 1)))
        for n, slot in enumerate(SLOT):
            index = index + jnp.where(turn == n, slot, 0)
        hit = hit + jnp.where(r == index, 1.0, 0.0)
    hit = hit.astype(jnp.bfloat16)
    first = jnp.where(chosen, (number + 1).astype(jnp.float32), 0.0).astype(jnp.bfloat16)
    second = jnp.where(chosen, shift + 1.0, 0.0).astype(jnp.bfloat16)
    listed[...] = jnp.dot(hit, first, preferred_element_type=jnp.float32).astype(jnp.int32) - 1
    start = jnp.dot(hit, second, preferred_element_type=jnp.float32).astype(jnp.int32)
    goals = jnp.where(start > 0, start - 1 + ((lane & 31) >> 1) + TR * (lane & 1), -1)
    for n in range(2 * NT):
        koff_ref[n] = goals[n : n + 1, :]
    table_copy = pltpu.make_async_copy(listed, table, table_sem)
    table_copy.start()

    pl.semaphore_wait(barrier, len(peers))

    def remote(src, dst, ssem, rsem, dev):
        return pltpu.make_async_remote_copy(
            src_ref=src, dst_ref=dst, send_sem=ssem, recv_sem=rsem, device_id=dev, device_id_type=MESH
        )

    def way_of(q):
        return 1 - 2 * (q % 2 if isinstance(q, int) else lax.rem(q, 2))

    def koff_copies(par):
        copies = []
        for k in (2, 1, 3):
            there = lax.rem(x + k, NX)
            copies.append(remote(
                koff_ref.at[pl.ds(par * NT + there * NZ, 6)], kof.at[par, x, pl.ds(0, 6)],
                ks_sem.at[par, k], kr_sem.at[par, k], at(k, 0),
            ))
        for m, way in ((6, 1 - 2 * par), (7, 2 * par - 1)):
            for k in range(NX):
                there, n = lax.rem(x + k, NX), 4 * (m - 5) + k
                copies.append(remote(
                    koff_ref.at[par * NT + there * NZ + m], kof.at[par, x, m],
                    ks_sem.at[par, n], kr_sem.at[par, n], at(k, way),
                ))
        return copies

    def x_group(q, g):
        rows = pl.ds(pl.multiple_of(x * KP, KP), KS)
        copies = []
        if g > 0:
            for k in (2, 1, 3):
                first, n = lax.rem(x + k, NX) * NZ + 2 * g - 2, 8 + 4 * g + k
                copies.append(remote(
                    zb.at[q, pl.ds(first, 2)], got.at[q, pl.ds(2 * g - 2, 2), rows],
                    xs_sem.at[q, n], xr_sem.at[q, n], at(k, 0),
                ))
            return copies
        for m, way in ((6, way_of(q)), (7, -way_of(q))):
            for k in range(NX):
                there, n = lax.rem(x + k, NX), 4 * (m - 5) + k
                copies.append(remote(
                    zb.at[q, there * NZ + m], got.at[q, m, rows],
                    xs_sem.at[q, n], xr_sem.at[q, n], at(k, way),
                ))
        return copies

    def own_copy(q):
        return pltpu.make_async_copy(
            zb.at[q, pl.ds(x * NZ, 6)], got.at[q, pl.ds(0, 6), pl.ds(pl.multiple_of(x * KP, KP), KS)],
            own_sem.at[q],
        )

    for par in range(2):
        for copy in koff_copies(par):
            copy.start()
    table_copy.wait()
    load(0).wait()
    blocks0 = held0.reshape(BLK, 2 * BR, 128)
    blocks = held.reshape((NQ - 1) * BLK, 2 * BR, 128)

    def send_blocks(q, source, first):
        par = q % 2 if isinstance(q, int) else lax.rem(q, 2)

        @pl.loop(0, NT)
        def _(i):
            for k in range(CAP):
                b = table[par * NT + i, k * 32]
                v = source[first + jnp.minimum(jnp.maximum(b, 0), BLK - 1)]
                zb[q, i, k * 32 : (k + 1) * 32, :] = jnp.where(b >= 0, v, jnp.zeros_like(v))

        for g in range(4):
            for copy in x_group(q, g):
                copy.start()
        own_copy(q).start()

    def build(par):
        kof[par, x, 0:6] = koff_ref[pl.ds(par * NT + x * NZ, 6)]
        for copy in koff_copies(par):
            copy.wait()

        @pl.loop(0, NZ)
        def _(j):
            for s in range(NX):
                goal = kof[par, s, j]
                for i in range(4):
                    row = lax.broadcasted_iota(jnp.int32, (128, 128), 0) + i * 128
                    hit = jnp.where(row == goal, 1.0, 0.0).astype(jnp.bfloat16)
                    place[par, j, i * 128 : (i + 1) * 128, s * 128 : (s + 1) * 128] = hit

    send_blocks(0, blocks0, 0)
    for q in range(1, NQ):
        load(q).wait()

    @pl.loop(1, 3)
    def _(q):
        send_blocks(q, blocks, (q - 1) * BLK)

    build(0)
    build(1)
    for half in range(2):
        i = lax.broadcasted_iota(jnp.int32, (256, 256), 0)
        j = lax.broadcasted_iota(jnp.int32, (256, 256), 1)
        near = jnp.abs((i & 127) + half * 128 - j) <= 7
        bands[half] = jnp.where(near, 1.0, 0.0).astype(jnp.bfloat16)
    prod[...] = jnp.zeros_like(prod)

    def part(q, j, i):
        return jnp.dot(
            place[lax.rem(q, 2), j, i * 128 : (i + 1) * 128, :], got[q, j],
            preferred_element_type=jnp.float32,
        )

    def z_copy(q, n, h, way):
        piece = pl.ds(h * PIECE, PIECE if h == 0 else TR)
        return remote(
            sent.at[q, n, piece], came.at[q, n, piece], zs_sem.at[q, 2 * n + h], zr_sem.at[q, 2 * n + h], at(0, way)
        )

    def own_part(q, slots, at_total):
        top = jnp.zeros((8, 128), jnp.float32)
        for i in range(4):
            v = part(q, slots[0], i)
            for slot in slots[1:]:
                v = v + part(q, slot, i)
            total[at_total, i * 128 : (i + 1) * 128, :] = v
            top = jnp.maximum(top, jnp.max(jnp.abs(v).reshape(16, 8, 128), axis=0))
        return jnp.max(top, axis=0, keepdims=True)

    def hop(q, units):
        tops = [own_part(q, slots, u) for u, (_, slots, _, _) in enumerate(units)]
        scales = [None] * len(units)
        for h in range(2):
            for u, (way, _, taken, n) in enumerate(units):
                if taken is not None:
                    z_copy(q, taken, h, way).wait_recv()
                if h == 0:
                    arrived = None
                    if taken is not None:
                        arrived = scale_of(came[q, taken, 2 * 128 : PIECE, :])
                        tops[u] = tops[u] + arrived
                    power = power_of(tops[u])
                    sent[q, n, 2 * 128 : PIECE, :] = (
                        jnp.broadcast_to(power, (16, 128)).astype(jnp.int32).astype(jnp.int16)
                    )
                    scales[u] = (arrived, jnp.exp2(-power))
                arrived, scale = scales[u]
                for part_no in range(2):
                    i = part_no * 2 + h
                    rows = slice(h * PIECE + part_no * 128, h * PIECE + part_no * 128 + 128)
                    v = total[u, i * 128 : (i + 1) * 128, :]
                    if taken is not None:
                        v = v + decode(came[q, taken, rows, :], arrived)
                    sent[q, n, rows, :] = encode(v, scale)
                z_copy(q, n, h, way).start()

    def y_copy(fall, q, k, h):
        mine = fall.at[d * 4 + lax.rem(q, 4), :, pl.ds(h * 128, 128)]
        n = 2 * k - 2 + h
        return remote(mine, mine, ys_sem.at[q, n], yr_sem.at[q, n], at_y(k))

    def core_copy(fall, q, k, h):
        from_d = lax.rem(y - k + NY, NY) * 2 + core
        field = fall.at[from_d * 4 + lax.rem(q, 4), :, pl.ds(h * 128, 128)]
        return remote(field, field, cs_sem.at[q, 2 * k + h], cr_sem.at[q, 2 * k + h], partner)

    def finish(q, fall):
        way = way_of(q)
        own_part(q, (5,), 0)
        scales = [None, None]
        for h in range(2):
            for u, (n, w) in enumerate(((2, way), (4, -way))):
                z_copy(q, n, h, w).wait_recv()
                if h == 0:
                    scales[u] = scale_of(came[q, n, 2 * 128 : PIECE, :])
            for part_no in range(2):
                i = part_no * 2 + h
                rows = slice(h * PIECE + part_no * 128, h * PIECE + part_no * 128 + 128)
                v = total[0, i * 128 : (i + 1) * 128, :]
                v = v + (decode(came[q, 2, rows, :], scales[0]) + decode(came[q, 4, rows, :], scales[1]))
                fall[d * 4 + lax.rem(q, 4), part_no, h * 128 : (h + 1) * 128, :] = v.astype(jnp.bfloat16)
            for k in (2, 1, 3):
                y_copy(fall, q, k, h).start()
            core_copy(fall, q, 0, h).start()

    def forward(q, fall):
        for h in range(2):
            for k in (2, 1, 3):
                y_copy(fall, q, k, h).wait_recv()
                core_copy(fall, q, k, h).start()

    def arrive(q, fall):
        for h in range(2):
            for k in range(NY):
                core_copy(fall, q, k, h).wait_recv()

    def out_copy(side):
        return pltpu.make_async_copy(
            result.reshape(2, TR, NP, 128).at[side],
            out_ref.at[:, :, pl.ds(side * 128, 128)],
            out_sem.at[side],
        )

    def boxes(half, fall, first, number):
        @pl.loop(first, first + number)
        def _(p):
            a = ep_ref[0, d * NP + p]
            e = ep_ref[1, d * NP + p]
            for i in range(4):
                lo = i * 64
                u0 = fall[a, 0, lo : lo + 64, :].astype(jnp.float32)
                u1 = fall[a, 1, lo : lo + 64, :].astype(jnp.float32)
                v0 = fall[e, 0, lo : lo + 64, :].astype(jnp.float32)
                v1 = fall[e, 1, lo : lo + 64, :].astype(jnp.float32)
                prod[0, 8 + lo : 72 + lo, :] = u0 * v0 + u1 * v1
                prod[1, 8 + lo : 72 + lo, :] = u1 * v0 - u0 * v1
                prod[2, 8 + lo : 72 + lo, :] = u0 * u0 + u1 * u1
                prod[3, 8 + lo : 72 + lo, :] = v0 * v0 + v1 * v1
            for f in range(4):
                for i in range(4):
                    lo = i * 64
                    s = prod[f, 5 + lo : 69 + lo, :]
                    for k in range(1, 7):
                        s = s + prod[f, 5 + lo + k : 69 + lo + k, :]
                    high = s.astype(jnp.bfloat16)
                    low = (s - high.astype(jnp.float32)).astype(jnp.bfloat16)
                    split[f, lo : lo + 64, 0:128] = high
                    split[f, lo : lo + 64, 128:256] = low
            for f in range(4):
                r = jnp.dot(split[f], bands[half], preferred_element_type=jnp.float32)
                acc[p, f] = r if half == 0 else acc[p, f] + r
            if half == 1:
                for i in range(8):
                    lo = i * 32
                    re, im, pa, pe = [acc[p, f, lo : lo + 32, :] for f in range(4)]
                    n = re * re + im * im
                    c = n * lax.rsqrt(jnp.maximum(n, 1e-30)) * lax.rsqrt(jnp.maximum(pa * pe, 1.0))
                    for side in range(2):
                        rows = pl.ds(side * NP * TR + lo * NP + p, 32, stride=NP)
                        result[rows, :] = c[:, side * 128 : (side + 1) * 128]

    @pl.loop(0, NQ + 3)
    def _(step):
        @pl.when(step < NQ)
        def _():
            for copy in x_group(step, 0) + x_group(step, 1):
                copy.wait_recv()
            own_copy(step).wait()
            hop(step, ((way_of(step), (1, 6), None, 0), (-way_of(step), (0, 7), None, 3)))

        @pl.when((step >= 1) & (step < NQ + 1))
        def _():
            for copy in x_group(step - 1, 3):
                copy.wait_recv()
            hop(step - 1, ((way_of(step - 1), (4,), 1, 2),))

        @pl.when(step + 3 < NQ)
        def _():
            send_blocks(step + 3, blocks, (step + 2) * BLK)

        for half, fall in enumerate((fall0, fall1)):
            first = half * 4

            @pl.when((step >= first + 2) & (step < first + 6))
            def _(fall=fall):
                forward(step - 2, fall)

            @pl.when((step >= first + 3) & (step < first + 7))
            def _(fall=fall):
                arrive(step - 3, fall)

        @pl.when(step < NQ)
        def _():
            for copy in x_group(step, 2):
                copy.wait_recv()
            hop(step, ((way_of(step), (2,), 0, 1), (-way_of(step), (3,), 3, 4)))

        for half, fall in enumerate((fall0, fall1)):
            first = half * 4

            @pl.when((step >= first + 1) & (step < first + 5))
            def _(fall=fall):
                finish(step - 1, fall)

        @pl.when((step == 6) | (step == 8))
        def _():
            boxes(0, fall0, (step - 6) * 2, 4)

    boxes(1, fall1, 0, NP)
    for side in range(2):
        out_copy(side).start()

    @pl.loop(0, NQ)
    def _(q):
        for g in range(4):
            for copy in x_group(q, g):
                copy.wait_send()
        for h in range(2):
            for n in range(5):
                z_copy(q, n, h, 1).wait_send()
            for k in (1, 2, 3):
                y_copy(fall0, q, k, h).wait_send()
            for k in range(NY):
                core_copy(fall0, q, k, h).wait_send()

    for side in range(2):
        out_copy(side).wait()


def main_call(dest, shift, epochs, x):
    dma = pltpu.SemaphoreType.DMA
    field = pltpu.VMEM((32, 2, TR, 128), jnp.bfloat16)
    vmem = pl.BlockSpec(memory_space=pltpu.VMEM)
    return pl.pallas_call(
        main_kernel,
        out_shape=jax.ShapeDtypeStruct((TR, NP, 256), jnp.float32),
        in_specs=[vmem, vmem, pl.BlockSpec(memory_space=pltpu.SMEM), pl.BlockSpec(memory_space=pl.ANY)],
        out_specs=pl.BlockSpec(memory_space=pl.ANY),
        scratch_shapes=[
            pltpu.SMEM((2 * NT, 128), jnp.int32),
            pltpu.VMEM((2 * NT, 128), jnp.int32),
            pltpu.VMEM((2 * NT, 1, 128), jnp.int32),
            pltpu.VMEM((BLK, BR, 2, 128), jnp.bfloat16),
            pltpu.VMEM(((NQ - 1) * BLK, BR, 2, 128), jnp.bfloat16),
            pltpu.VMEM((NQ, NT, KS, 128), jnp.bfloat16),
            pltpu.VMEM((NQ, NZ, NX * KP, 128), jnp.bfloat16),
            pltpu.VMEM((2, NX, NZ, 1, 128), jnp.int32),
            pltpu.VMEM((2, NZ, 2 * TR, NX * KP), jnp.bfloat16),
            pltpu.VMEM((NQ, 5, MSG, 128), jnp.int16),
            pltpu.VMEM((NQ, 5, MSG, 128), jnp.int16),
            pltpu.VMEM((2, 2 * TR, 128), jnp.float32),
            field,
            field,
            pltpu.VMEM((4, TR + 16, 128), jnp.float32),
            pltpu.VMEM((4, TR, 256), jnp.bfloat16),
            pltpu.VMEM((NP, 4, TR, 256), jnp.float32),
            pltpu.VMEM((2, 256, 256), jnp.bfloat16),
            pltpu.VMEM((2 * TR * NP, 128), jnp.float32),
            dma((NQ,)), dma((NQ,)),
            dma((NQ, 24)), dma((NQ, 24)),
            dma((NQ, 10)), dma((NQ, 10)),
            dma((NQ, 6)), dma((NQ, 6)),
            dma((NQ, 2 * NY)), dma((NQ, 2 * NY)),
            dma((2, 12)), dma((2, 12)),
            dma((2,)),
            dma,
        ],
        compiler_params=pltpu.CompilerParams(
            collective_id=0, has_side_effects=True, vmem_limit_bytes=58 * 2**20
        ),
        name="tiles_and_coherence",
    )(dest, shift, epochs, x)


def local(radar_echoes, destination_panel, panel_line_shift, epoch_couples):
    dest, shift = destination_panel.reshape(1, BLK), panel_line_shift.reshape(1, BLK)
    return main_call(dest, shift, epoch_couples.T, radar_echoes)


def solution(mesh):
    in_specs = (P("tile", None, "date", None, None), P("tile", None), P("tile"), P())
    out_specs = P("tile", "date", None)
    return jax.shard_map(local, mesh=mesh, in_specs=in_specs, out_specs=out_specs, check_vma=False)
```
